512 devices in a mesh: node: 32 (over z, x_lo, core), local: 16 (over x_hi, y).
Axes of the slice: x: 4 (x_hi: 2, x_lo: 2; x = x_hi * 2 + x_lo), y: 8, z: 8, core: 2. Of those that a mesh axis runs over, the one named last changes fastest.
Arguments:
- tokens: bfloat16 [2048, 4096], P('local', 'node'), may hold values from -6 to 6
- gate_up_codes: bfloat16 [2, 4096, 14336], P(None, 'local', 'node'), may hold values from -127 to 127
- gate_up_scales: bfloat16 [2, 32, 14336], P(None, 'local', 'node'), may hold values from 2.9921532e-05 to 0.00029945374
- d_hidden: bfloat16 [2048, 14336], P('local', 'node'), may hold values from -6 to 6
Outputs:
- hidden: bfloat16 [2048, 14336], P('local', 'node')
- d_tokens: bfloat16 [2048, 4096], P('local', 'node')
- grad_gate_up: float32 [2, 4096, 14336], P(None, 'local', 'node')
The draws below stay inside these ranges and needn't reach their ends.
All inputs are finite; a program needn't handle non-finite values.
Results may differ from the reference program's by a relative error of at most 0.023.
Values may be sent and summed in bfloat16 or wider, within the bound.
A program may use at most 128 MiB of HBM per device.

```python
import math
import jax
import jax.numpy as jnp
from jax import lax

D = 4096
FF = 14336
BLOCK = 128
TOK_DEV = 128
TOKENS = 2048
N_NODE = 32
N_LOCAL = 16


def level_of(rng, shape, shards, low, largest):
    gain = 1.0
    for position, blocks in shards:
        heights = jax.random.uniform(jax.random.fold_in(jax.random.fold_in(rng, 6), position), (blocks,), jnp.float32, low / len(shards), largest / len(shards))
        gain = gain * jnp.repeat(jnp.exp(heights), shape[position] // blocks).reshape((-1,) + (1,) * (len(shape) - 1 - position))
    return gain


def gaussian(rng, extent, deviation, most, cuts=(), kind=jnp.bfloat16):
    entries = deviation * jax.random.normal(rng, extent, jnp.float32)
    if cuts:
        entries = entries * level_of(rng, extent, cuts, -0.22, 0.18)
    return jnp.clip(entries, -most, most).astype(kind)


def setup_inputs(seed: int = 0) -> dict:
    key_of = jax.random.split(jax.random.key(seed), 5)
    return {
        "tokens": gaussian(key_of[0], (TOKENS, D), 1.0, 6.0, ((0, 16), (1, 32))),
        "gate_up_codes": jnp.clip(jax.random.uniform(key_of[1], (2, D, FF), jnp.float32, -127.0, 127.0) * level_of(key_of[1], (2, D, FF), ((1, 16), (2, 32)), -0.4, 0.0), -127.0, 127.0).astype(jnp.bfloat16),
        "gate_up_scales": jnp.clip(jnp.exp(math.log(0.00029945374) - 2.3033816 * jax.random.uniform(key_of[2], (2, D // BLOCK, FF), jnp.float32) ** level_of(key_of[2], (2, D // BLOCK, FF), ((1, 16), (2, 32)), -0.2, 0.2)), 2.9921531677246094e-05, 0.00029945374).astype(jnp.bfloat16),
        "d_hidden": gaussian(key_of[3], (TOKENS, FF), 1.0, 6.0, ((0, 16), (1, 32))),
    }


def dequant(codes, scales):
    shape = codes.shape
    blocked = codes.astype(jnp.float32).reshape(shape[:-2] + (shape[-2] // BLOCK, BLOCK, shape[-1]))
    weight = blocked * scales.astype(jnp.float32)[..., :, None, :]
    return weight.reshape(shape).astype(jnp.bfloat16)

def reference(tokens, gate_up_codes, gate_up_scales, d_hidden):
    w_gu = dequant(gate_up_codes, gate_up_scales)
    gate = jnp.dot(tokens, w_gu[0], preferred_element_type=jnp.float32)
    up = jnp.dot(tokens, w_gu[1], preferred_element_type=jnp.float32)
    sigmoid_gate = jax.nn.sigmoid(gate)
    active = gate * sigmoid_gate
    hidden = (active * up).astype(jnp.bfloat16)
    grad_in = d_hidden.astype(jnp.float32)
    d_gate = (grad_in * up * sigmoid_gate * (1.0 + gate * (1.0 - sigmoid_gate))).astype(jnp.bfloat16)
    d_up = (grad_in * active).astype(jnp.bfloat16)
    group = FF // N_NODE
    gate_groups = d_gate.reshape(TOKENS, N_NODE, group).transpose(1, 0, 2)
    up_groups = d_up.reshape(TOKENS, N_NODE, group).transpose(1, 0, 2)
    wg_groups = w_gu[0].reshape(D, N_NODE, group).transpose(1, 0, 2)
    wu_groups = w_gu[1].reshape(D, N_NODE, group).transpose(1, 0, 2)

    def node_step(carry, pieces):
        dg, du, wg, wu = pieces
        term = lax.dot_general(dg, wg, (((1,), (1,)), ((), ())), preferred_element_type=jnp.float32)
        term = term + lax.dot_general(du, wu, (((1,), (1,)), ((), ())), preferred_element_type=jnp.float32)
        rounded = lax.optimization_barrier(term.astype(jnp.bfloat16))
        return (carry + rounded.astype(jnp.float32), None)
    token_sum, _ = lax.scan(node_step, jnp.zeros((TOKENS, D), jnp.float32), (gate_groups, up_groups, wg_groups, wu_groups))
    d_tokens = token_sum.astype(jnp.bfloat16)
    factor = 1.0 / math.sqrt(TOKENS)
    xs = tokens.reshape(N_LOCAL, TOK_DEV, D)
    gs = d_gate.reshape(N_LOCAL, TOK_DEV, FF)
    us = d_up.reshape(N_LOCAL, TOK_DEV, FF)

    def block_step(carry, pieces):
        rows, dg, du = pieces
        first = lax.dot_general(rows, dg, (((0,), (0,)), ((), ())), preferred_element_type=jnp.float32)
        second = lax.dot_general(rows, du, (((0,), (0,)), ((), ())), preferred_element_type=jnp.float32)
        partial_value = lax.optimization_barrier(jnp.stack([first, second]).astype(jnp.bfloat16))
        return (carry + partial_value.astype(jnp.float32), None)
    grads, _ = lax.scan(block_step, jnp.zeros((2, D, FF), jnp.float32), (xs, gs, us))
    return (hidden, d_tokens, grads * factor)
```

```python
import math

import jax
import jax.numpy as jnp
from jax import lax
from jax.experimental import pallas as pl
from jax.experimental.pallas import tpu as pltpu
from jax.sharding import PartitionSpec as P

MESH = pl.DeviceIdType.MESH
BLOCK = 128
NY = 8
NZ = 8
CHUNKS = 4
F32 = jnp.float32
BF16 = jnp.bfloat16


def dot_nn(a, b):
    return lax.dot_general(a, b, (((1,), (0,)), ((), ())), preferred_element_type=F32)


def dot_nt(a, b):
    return lax.dot_general(a, b, (((1,), (1,)), ((), ())), preferred_element_type=F32)


def kernel(
    tok_ref,
    codes_ref,
    scale_ref,
    dh_ref,
    hid_ref,
    dtok_ref,
    grad_ref,
    xin,
    x,
    w,
    wt,
    rs0,
    rs,
    part,
    own,
    dg,
    acc,
    dp,
    sib,
    zin,
    zsum,
    dtin,
    gsend,
    grecv,
    loc_sem,
    w_s,
    w_r,
    xg_s,
    xg_r,
    xp_s,
    xp_r,
    xm_s,
    xm_r,
    xs_s,
    xs_r,
    rs_s,
    rs_r,
    ag_s,
    ag_r,
    sb_s,
    sb_r,
    zl_s,
    zl_r,
    zs_s,
    zs_r,
    dt_s,
    dt_r,
    g_s,
    g_r,
):
    n = lax.axis_index("node")
    l = lax.axis_index("local")
    z = lax.div(n, 4)
    xl = lax.rem(lax.div(n, 2), 2)
    c = lax.rem(n, 2)
    h = lax.div(l, NY)
    y = lax.rem(l, NY)
    half = codes_ref.shape[1] // CHUNKS
    rows = 2 * half

    def dev(z_, xl_, c_, h_, y_):
        return (z_ * 4 + xl_ * 2 + c_, h_ * NY + y_)

    zu = lax.rem(z + 1, NZ)
    zd = lax.rem(z + NZ - 1, NZ)
    yu = lax.rem(y + 1, NY)
    yd = lax.rem(y + NY - 1, NY)
    up_z = dev(zu, xl, c, h, y)
    dn_z = dev(zd, xl, c, h, y)
    up_y = dev(z, xl, c, h, yu)
    dn_y = dev(z, xl, c, h, yd)
    sibling = dev(z, xl, 1 - c, h, y)
    partner = dev(z, xl, c, 1 - h, y)
    other = 1 - c

    barrier = pltpu.get_barrier_semaphore()
    peers = [up_z, dn_z, sibling, partner]
    for dx in range(2):
        for dy in range(NY):
            if dx or dy:
                peers.append(dev(z, lax.rem(xl + dx, 2), c, h, lax.rem(y + dy, NY)))
    for peer in peers:
        pl.semaphore_signal(barrier, inc=1, device_id=peer, device_id_type=MESH)

    def remote(src, dst, ss, rr, to):
        return pltpu.make_async_remote_copy(
            src_ref=src, dst_ref=dst, send_sem=ss, recv_sem=rr, device_id=to, device_id_type=MESH
        )

    for k in range(2):
        for i in range(CHUNKS):
            f = pl.ds(half * i, half)
            code = codes_ref[k, f, :].astype(F32)
            sc = scale_ref[k, f, :]
            s = jnp.concatenate(
                [jnp.broadcast_to(sc[:, b : b + 1], (half, BLOCK)) for b in range(2)], axis=1
            )
            w[h, pl.ds(rows * i + half * k, half), :] = (code * s).astype(BF16)
    xin[...] = tok_ref[...]

    pl.semaphore_wait(barrier, len(peers))

    wcopy = remote(w.at[h], w.at[h], w_s, w_r, partner)
    wcopy.start()

    ystar = 2 * lax.rem(z, 4) + xl
    qsrc = lax.div(z, 4)
    myslot = x.at[2 * qsrc + c, y]
    own_col = dev(z, xl, c, h, ystar)
    oth_col = dev(z, 1 - xl, c, h, ystar)
    xg0 = remote(xin, myslot, xg_s.at[0], xg_r.at[y], own_col)
    xg1 = remote(xin, myslot, xg_s.at[1], xg_r.at[y], oth_col)
    xg1.start()
    selfcol = ystar == y

    @pl.when(selfcol)
    def _():
        pltpu.make_async_copy(xin, myslot, xg_r.at[y]).start()

    @pl.when(jnp.logical_not(selfcol))
    def _():
        xg0.start()

    dz = lax.rem(z - lax.div(y, 2) + NZ, NZ)
    r = lax.rem(dz, 4)
    qo = lax.div(dz, 4)
    qp = lax.div(lax.rem(dz + 7, NZ), 4)
    qm = 1 - qp

    def block(d):
        return lax.rem(y + d + NY, NY)

    order = [block(d) for d in (4, 3, -3, 2, -2, 1, -1, 0)]

    def slot(q, tb):
        return x.at[2 * q + c, tb]

    def cp_plus(q, i):
        s = slot(q, order[i])
        return remote(s, s, xp_s.at[i], xp_r.at[i], up_z)

    def cp_minus(q, i):
        s = slot(q, order[i])
        return remote(s, s, xm_s.at[i], xm_r.at[i], dn_z)

    def cp_sib(q, i):
        s = slot(q, order[i])
        return remote(s, s, xs_s.at[q, i], xs_r.at[q, i], sibling)

    @pl.when(r == 0)
    def _():
        for i in range(NY):
            s = slot(qo, order[i])
            remote(xin, s, xg_s.at[0], xg_r.at[order[i]], own_col).wait_recv()
            cp_plus(qo, i).start()
            cp_minus(qo, i).start()
            cp_sib(qo, i).start()
        for i in range(NY):
            cp_plus(qp, i).wait_recv()
            cp_sib(qp, i).start()

    @pl.when(r == 1)
    def _():
        for i in range(NY):
            cp_plus(qp, i).wait_recv()
            cp_plus(qp, i).start()
            cp_sib(qp, i).start()
        for i in range(NY):
            cp_minus(qm, i).wait_recv()
            cp_sib(qm, i).start()

    @pl.when(r == 2)
    def _():
        for i in range(NY):
            cp_plus(qp, i).wait_recv()
            cp_plus(qp, i).start()
            cp_sib(qp, i).start()
            cp_minus(qm, i).wait_recv()
            cp_minus(qm, i).start()
            cp_sib(qm, i).start()

    @pl.when(r == 3)
    def _():
        for i in range(NY):
            cp_minus(qm, i).wait_recv()
            cp_minus(qm, i).start()
            cp_sib(qm, i).start()
        for i in range(NY):
            cp_plus(qp, i).wait_recv()
            cp_plus(qp, i).start()
            cp_sib(qp, i).start()

    for q in range(2):
        for i in range(NY):
            s = x.at[2 * q + other, order[i]]
            remote(s, s, xs_s.at[q, i], xs_r.at[q, i], sibling).wait_recv()

    remote(w.at[1 - h], w.at[1 - h], w_s, w_r, partner).wait_recv()

    def xq(q, tb):
        return jnp.concatenate([x[2 * q, tb], x[2 * q + 1, tb]], axis=1)

    def partial(tb, lo, hi):
        a = slice(lo * rows, hi * rows)
        return dot_nt(w[0, a, :], xq(0, tb)) + dot_nt(w[1, a, :], xq(1, tb))

    def ch(i):
        return pl.ds(rows * i, rows)

    nbr = (up_y, dn_y)
    hc = CHUNKS // 2

    def rs_copy(s, d, i):
        src = rs0.at[d, ch(i - hc * d)] if s == 0 else rs.at[d, s - 1, ch(i)]
        return remote(src, rs.at[d, s, ch(i)], rs_s.at[s, d, i], rs_r.at[s, d, i], nbr[d])

    def firsts(d):
        return range(hc) if d == 0 else range(hc, CHUNKS)

    p0 = partial(block(4), 0, CHUNKS)
    for d in range(2):
        rs0[d] = p0[d * hc * rows : (d + 1) * hc * rows].astype(BF16)
        for i in firsts(d):
            rs_copy(0, d, i).start()
    for s in range(1, 4):
        for d in range(2):
            part[d] = partial(block(4 - s if d == 0 else s - 4), 0, CHUNKS)
        if s == 1:
            for d in range(2):
                for i in firsts(1 - d):
                    rs[d, 0, ch(i)] = part[d, ch(i)].astype(BF16)
                    rs_copy(1, d, i).start()
        for i in range(CHUNKS):
            for d in range(2):
                if s == 1:
                    if i not in firsts(d):
                        continue
                rs_copy(s - 1, d, i).wait_recv()
                rs[d, s - 1, ch(i)] = (rs[d, s - 1, ch(i)].astype(F32) + part[d, ch(i)]).astype(BF16)
                rs_copy(s, d, i).start()
    own[...] = partial(y, 0, CHUNKS)

    def ag_copy(s, d, i):
        b = lax.rem(y + (NY - s if d == 0 else s), NY)
        sl = dg.at[b, ch(i)]
        return remote(sl, sl, ag_s.at[s, d, i], ag_r.at[s, d, i], nbr[d])

    def ag_wait(s, d, i):
        b = lax.rem(y + (NY - 1 - s if d == 0 else s + 1), NY)
        sl = dg.at[b, ch(i)]
        remote(sl, sl, ag_s.at[s, d, i], ag_r.at[s, d, i], nbr[d]).wait_recv()

    for i in range(CHUNKS):
        for d in range(2):
            rs_copy(3, d, i).wait_recv()
        tot = own[ch(i)] + rs[0, 3, ch(i)].astype(F32) + rs[1, 3, ch(i)].astype(F32)
        gate, up = tot[:half], tot[half:]
        f = pl.ds(half * i, half)
        sg = jax.nn.sigmoid(gate)
        act = gate * sg
        hid_ref[f, :] = (act * up).astype(BF16)
        gin = dh_ref[f, :].astype(F32)
        dgate = (gin * up * sg * (1.0 + gate * (1.0 - sg))).astype(BF16)
        dup = (gin * act).astype(BF16)
        dg[y, pl.ds(rows * i, half), :] = dgate
        dg[y, pl.ds(rows * i + half, half), :] = dup
        for d in range(2):
            ag_copy(0, d, i).start()

    for q in range(2):
        wt[q] = jnp.transpose(w[q])

    def grads_of(blocks, first):
        a = jnp.concatenate([dg[b] for b in blocks], axis=1) if len(blocks) > 1 else dg[blocks[0]]
        for j in range(4):
            xs = [x[j, b] for b in blocks]
            bb = jnp.concatenate(xs, axis=0) if len(blocks) > 1 else xs[0]
            v = dot_nn(a, bb)
            col = slice(128 * (j % 2), 128 * (j % 2) + 128)
            if first:
                acc[j // 2, :, col] = v
            else:
                acc[j // 2, :, col] = acc[j // 2, :, col] + v

    def sib_copy(q, b, k):
        return remote(
            dp.at[2 * q + other, b], sib.at[q, k], sb_s.at[q, k], sb_r.at[q, k], sibling
        )

    def inputs_of(b, k):
        for q in range(2):
            v = dot_nn(wt[q], dg[b]).astype(BF16)
            dp[2 * q, b] = v[:128]
            dp[2 * q + 1, b] = v[128:]
            sib_copy(q, b, k).start()

    seq = [block(d) for d in (0, -1, 1, -2, 2, -3, 3, 4)]
    inputs_of(seq[0], 0)
    grads_of([seq[0]], True)
    for s in range(1, 5):
        for i in range(CHUNKS):
            for d in range(2):
                if s < 4 or i in firsts(d):
                    ag_wait(s - 1, d, i)
                if s < 3 or (s == 3 and i in firsts(d)):
                    ag_copy(s, d, i).start()
        if s < 4:
            inputs_of(seq[2 * s - 1], 2 * s - 1)
            inputs_of(seq[2 * s], 2 * s)
            grads_of([seq[2 * s - 1], seq[2 * s]], False)
        else:
            inputs_of(seq[7], 7)
            grads_of([seq[7]], False)

    gsend[...] = acc[1 - h].astype(BF16)
    gcopy = remote(gsend, grecv, g_s, g_r, partner)
    gcopy.start()

    for k in range(NY):
        for q in range(2):
            sib_copy(q, seq[k], k).wait_recv()
            v = dp[2 * q + c, seq[k]].astype(F32) + sib[q, k].astype(F32)
            zsum[q, k] = v.astype(BF16)

    def z_long(q, k):
        return remote(zsum.at[q, k], zin.at[0, k], zl_s.at[k], zl_r.at[k], dn_z)

    def z_short(q, k):
        return remote(zsum.at[q, k], zin.at[1, k], zs_s.at[k], zs_r.at[k], up_z)

    def long_hop(k):
        z_long(qp, k).wait_recv()
        zsum[qp, k] = (zsum[qp, k].astype(F32) + zin[0, k].astype(F32)).astype(BF16)
        z_long(qp, k).start()

    def short_hop(k):
        z_short(qm, k).wait_recv()
        zsum[qm, k] = (zsum[qm, k].astype(F32) + zin[1, k].astype(F32)).astype(BF16)
        z_short(qm, k).start()

    par = lax.rem(y, 2)

    @pl.when(r == 1)
    def _():
        for k in range(NY):
            z_short(qm, k).start()
        for k in range(NY):
            long_hop(k)

    @pl.when(r == 2)
    def _():
        for k in range(NY):
            short_hop(k)
            long_hop(k)

    @pl.when(r == 3)
    def _():
        for k in range(NY):
            long_hop(k)
        for k in range(NY):
            short_hop(k)

    def dt_copy(k, tb):
        return remote(
            zsum.at[qo, k], dtin.at[xl], dt_s.at[k], dt_r.at[xl], dev(z, par, c, h, tb)
        )

    mine = jnp.logical_and(r == 0, xl == par)

    @pl.when(r == 0)
    def _():
        for k in range(NY):
            z_long(qp, k).start()
        for k in range(NY):
            z_long(qp, k).wait_recv()
            z_short(qm, k).wait_recv()
            zsum[qo, k] = (
                zsum[qo, k].astype(F32) + zin[0, k].astype(F32) + zin[1, k].astype(F32)
            ).astype(BF16)
            if k > 0:
                dt_copy(k, seq[k]).start()
            else:

                @pl.when(xl == par)
                def _():
                    pltpu.make_async_copy(zsum.at[qo, 0], dtin.at[xl], dt_r.at[xl]).start()

                @pl.when(xl != par)
                def _():
                    dt_copy(0, seq[0]).start()

    remote(gsend, grecv, g_s, g_r, partner).wait_recv()
    for i in range(CHUNKS):
        for k in range(2):
            a = pl.ds(rows * i + half * k, half)
            grad_ref[k, pl.ds(half * i, half), :] = acc[h, a, :] + grecv[a, :].astype(F32)

    for s in range(2):
        remote(zsum.at[0, 0], dtin.at[s], dt_s.at[0], dt_r.at[s], sibling).wait_recv()
    tot = dtin[0].astype(F32) + dtin[1].astype(F32)
    dtok_ref[...] = jnp.transpose(tot).astype(BF16)

    wcopy.wait_send()
    xg1.wait_send()

    @pl.when(jnp.logical_not(selfcol))
    def _():
        xg0.wait_send()

    for i in range(NY):
        cp_plus(0, i).wait_send()
        for q in range(2):
            cp_sib(q, i).wait_send()

    @pl.when(r != 1)
    def _():
        for i in range(NY):
            cp_minus(0, i).wait_send()

    for s in range(4):
        for d in range(2):
            for i in range(CHUNKS):
                if s > 0 or i in firsts(d):
                    rs_copy(s, d, i).wait_send()
                if s < 3 or i in firsts(d):
                    ag_copy(s, d, i).wait_send()
    for k in range(NY):
        for q in range(2):
            sib_copy(q, seq[k], k).wait_send()
        z_long(0, k).wait_send()

    @pl.when(r != 0)
    def _():
        for k in range(NY):
            z_short(0, k).wait_send()

    @pl.when(r == 0)
    def _():
        for k in range(1, NY):
            dt_copy(k, seq[k]).wait_send()

    @pl.when(jnp.logical_and(r == 0, xl != par))
    def _():
        dt_copy(0, seq[0]).wait_send()

    gcopy.wait_send()


def body(tokens, codes, scales, d_hidden):
    t, dloc = tokens.shape
    _, wrows, group = codes.shape
    all2 = 2 * group
    codes_t = jnp.transpose(codes, (0, 2, 1))
    scale_t = jnp.transpose(scales, (0, 2, 1)).astype(F32)
    dh_t = jnp.transpose(d_hidden)
    dma = pltpu.SemaphoreType.DMA
    vm = pl.BlockSpec(memory_space=pltpu.VMEM)
    hid_t, dtok, grad_t = pl.pallas_call(
        kernel,
        out_shape=(
            jax.ShapeDtypeStruct((group, t), BF16),
            jax.ShapeDtypeStruct((t, dloc), BF16),
            jax.ShapeDtypeStruct((2, group, wrows), F32),
        ),
        in_specs=[vm] * 4,
        out_specs=(vm, vm, vm),
        scratch_shapes=[
            pltpu.VMEM((t, dloc), BF16),
            pltpu.VMEM((4, NY, t, dloc), BF16),
            pltpu.VMEM((2, all2, wrows), BF16),
            pltpu.VMEM((2, wrows, all2), BF16),
            pltpu.VMEM((2, all2 // 2, t), BF16),
            pltpu.VMEM((2, 4, all2, t), BF16),
            pltpu.VMEM((2, all2, t), F32),
            pltpu.VMEM((all2, t), F32),
            pltpu.VMEM((NY, all2, t), BF16),
            pltpu.VMEM((2, all2, wrows), F32),
            pltpu.VMEM((4, NY, dloc, t), BF16),
            pltpu.VMEM((2, NY, dloc, t), BF16),
            pltpu.VMEM((2, NY, dloc, t), BF16),
            pltpu.VMEM((2, NY, dloc, t), BF16),
            pltpu.VMEM((2, dloc, t), BF16),
            pltpu.VMEM((all2, wrows), BF16),
            pltpu.VMEM((all2, wrows), BF16),
            dma(()),
            dma(()),
            dma(()),
            dma((2,)),
            dma((NY,)),
            dma((NY,)),
            dma((NY,)),
            dma((NY,)),
            dma((NY,)),
            dma((2, NY)),
            dma((2, NY)),
            dma((4, 2, CHUNKS)),
            dma((4, 2, CHUNKS)),
            dma((4, 2, CHUNKS)),
            dma((4, 2, CHUNKS)),
            dma((2, NY)),
            dma((2, NY)),
            dma((NY,)),
            dma((NY,)),
            dma((NY,)),
            dma((NY,)),
            dma((NY,)),
            dma((2,)),
            dma(()),
            dma(()),
        ],
        compiler_params=pltpu.CompilerParams(collective_id=0, has_side_effects=True),
    )(tokens, codes_t, scale_t, dh_t)
    factor = 1.0 / math.sqrt(t * lax.axis_size("local"))
    return (jnp.transpose(hid_t), dtok, jnp.transpose(grad_t, (0, 2, 1)) * factor)


def solution(mesh):
    return jax.shard_map(
        body,
        mesh=mesh,
        in_specs=(
            P("local", "node"),
            P(None, "local", "node"),
            P(None, "local", "node"),
            P("local", "node"),
        ),
        out_specs=(P("local", "node"), P("local", "node"), P(None, "local", "node")),
        check_vma=False,
    )
```

```python
import math

import jax
import jax.numpy as jnp
from jax import lax
from jax.experimental import pallas as pl
from jax.experimental.pallas import tpu as pltpu
from jax.sharding import PartitionSpec as P

MESH = pl.DeviceIdType.MESH
BLOCK = 128
NY = 8
NZ = 8
CHUNKS = 4
F32 = jnp.float32
BF16 = jnp.bfloat16


def dot_nn(a, b):
    return lax.dot_general(a, b, (((1,), (0,)), ((), ())), preferred_element_type=F32)


def dot_nt(a, b):
    return lax.dot_general(a, b, (((1,), (1,)), ((), ())), preferred_element_type=F32)


def kernel(
    tok_hbm,
    codes_hbm,
    scale_hbm,
    dh_hbm,
    hid_ref,
    dtok_ref,
    grad_ref,
    codes_ref,
    scale_ref,
    dh_ref,
    in_sem,
    xin,
    x,
    w,
    wt,
    rs0,
    rs,
    part,
    own,
    dg,
    acc,
    dp,
    sib,
    zin,
    zsum,
    dtin,
    gsend,
    grecv,
    loc_sem,
    w_s,
    w_r,
    xg_s,
    xg_r,
    xp_s,
    xp_r,
    xm_s,
    xm_r,
    xs_s,
    xs_r,
    rs_s,
    rs_r,
    ag_s,
    ag_r,
    sb_s,
    sb_r,
    zo_s,
    zo_r,
    dt_s,
    dt_r,
    g_s,
    g_r,
):
    loads = [
        pltpu.make_async_copy(a, b, in_sem.at[i])
        for i, (a, b) in enumerate(
            ((tok_hbm, xin), (scale_hbm, scale_ref), (codes_hbm, codes_ref), (dh_hbm, dh_ref))
        )
    ]
    for load in loads:
        load.start()

    n = lax.axis_index("node")
    l = lax.axis_index("local")
    z = lax.div(n, 4)
    xl = lax.rem(lax.div(n, 2), 2)
    c = lax.rem(n, 2)
    h = lax.div(l, NY)
    y = lax.rem(l, NY)
    half = codes_ref.shape[1] // CHUNKS
    factor = 1.0 / math.sqrt(tok_hbm.shape[0] * 16)
    rows = 2 * half

    def dev(z_, xl_, c_, h_, y_):
        return (z_ * 4 + xl_ * 2 + c_, h_ * NY + y_)

    zu = lax.rem(z + 1, NZ)
    zd = lax.rem(z + NZ - 1, NZ)
    yu = lax.rem(y + 1, NY)
    yd = lax.rem(y + NY - 1, NY)
    zu2 = lax.rem(z + 2, NZ)
    zd2 = lax.rem(z + NZ - 2, NZ)
    up_z = dev(zu, xl, c, h, y)
    up_z2 = dev(zu2, xl, c, h, y)
    dn_z2 = dev(zd2, xl, c, h, y)
    dn_z = dev(zd, xl, c, h, y)
    up_y = dev(z, xl, c, h, yu)
    dn_y = dev(z, xl, c, h, yd)
    sibling = dev(z, xl, 1 - c, h, y)
    partner = dev(z, xl, c, 1 - h, y)
    other = 1 - c

    barrier = pltpu.get_barrier_semaphore()
    peers = [up_z, dn_z, up_z2, dn_z2, sibling, partner]
    for dx in range(2):
        for dy in range(NY):
            if dx or dy:
                peers.append(dev(z, lax.rem(xl + dx, 2), c, h, lax.rem(y + dy, NY)))
    for peer in peers:
        pl.semaphore_signal(barrier, inc=1, device_id=peer, device_id_type=MESH)

    def remote(src, dst, ss, rr, to):
        return pltpu.make_async_remote_copy(
            src_ref=src, dst_ref=dst, send_sem=ss, recv_sem=rr, device_id=to, device_id_type=MESH
        )

    loads[1].wait()
    loads[2].wait()
    pick = (
        lax.broadcasted_iota(jnp.int32, (2, 2 * BLOCK), 1) // BLOCK
        == lax.broadcasted_iota(jnp.int32, (2, 2 * BLOCK), 0)
    ).astype(F32)
    for k in range(2):
        spread = lax.dot_general(
            scale_ref[k].astype(F32),
            pick,
            (((0,), (0,)), ((), ())),
            precision=lax.Precision.HIGHEST,
            preferred_element_type=F32,
        )
        for i in range(CHUNKS):
            f = pl.ds(half * i, half)
            code = codes_ref[k, f, :].astype(F32)
            s = spread[half * i : half * (i + 1)]
            w[h, pl.ds(rows * i + half * k, half), :] = (code * s).astype(BF16)
    loads[0].wait()
    loads[3].wait()

    pl.semaphore_wait(barrier, len(peers))

    wcopy = remote(w.at[h], w.at[h], w_s, w_r, partner)
    wcopy.start()

    ystar = 2 * lax.rem(z, 4) + xl
    qsrc = lax.div(z, 4)
    myslot = x.at[2 * qsrc + c, y]
    own_col = dev(z, xl, c, h, ystar)
    oth_col = dev(z, 1 - xl, c, h, ystar)
    xg0 = remote(xin, myslot, xg_s.at[0], xg_r.at[y], own_col)
    xg1 = remote(xin, myslot, xg_s.at[1], xg_r.at[y], oth_col)
    xg1.start()
    selfcol = ystar == y

    @pl.when(selfcol)
    def _():
        pltpu.make_async_copy(xin, myslot, xg_r.at[y]).start()

    @pl.when(jnp.logical_not(selfcol))
    def _():
        xg0.start()

    dz = lax.rem(z - lax.div(y, 2) + NZ, NZ)
    r = lax.rem(dz, 4)
    qo = lax.div(dz, 4)
    qp = lax.div(lax.rem(dz + 7, NZ), 4)
    qm = 1 - qp

    def block(d):
        return lax.rem(y + d + NY, NY)

    order = [block(d) for d in (4, 3, -3, 2, -2, 1, -1, 0)]

    def slot(q, tb):
        return x.at[2 * q + c, tb]

    def cp_plus(q, i, far):
        s = slot(q, order[i])
        return remote(s, s, xp_s.at[far, i], xp_r.at[i], up_z2 if far else up_z)

    def cp_minus(q, i, far):
        s = slot(q, order[i])
        return remote(s, s, xm_s.at[far, i], xm_r.at[i], dn_z2 if far else dn_z)

    def cp_sib(q, i):
        s = slot(q, order[i])
        return remote(s, s, xs_s.at[q, i], xs_r.at[q, i], sibling)

    def sib_wait(i):
        for q in range(2):
            s = x.at[2 * q + other, order[i]]
            remote(s, s, xs_s.at[q, i], xs_r.at[q, i], sibling).wait_recv()

    def spread_own(i):
        remote(xin, slot(qo, order[i]), xg_s.at[0], xg_r.at[order[i]], own_col).wait_recv()
        for far in (1, 0):
            cp_plus(qo, i, far).start()
            cp_minus(qo, i, far).start()
        cp_sib(qo, i).start()

    def take_plus(i):
        cp_plus(qp, i, 0).wait_recv()
        cp_sib(qp, i).start()

    def take_minus(i):
        cp_minus(qm, i, 0).wait_recv()
        cp_sib(qm, i).start()

    def relay(i):
        cp_plus(qp, i, 0).wait_recv()
        cp_plus(qp, i, 1).start()
        cp_plus(qp, i, 0).start()
        cp_sib(qp, i).start()
        cp_minus(qm, i, 0).wait_recv()
        cp_minus(qm, i, 0).start()
        cp_sib(qm, i).start()

    stages = ((0,), (1, 2), (3, 4), (5, 6, 7))
    early = ((0, 1, 2), (3, 4), (5, 6), (7,))

    def tokens_stage(t):
        @pl.when(r == 0)
        def _():
            if t == 0:
                for i in range(NY):
                    spread_own(i)
            for i in stages[t]:
                take_plus(i)

        @pl.when(r == 1)
        def _():
            for i in early[t]:
                take_plus(i)
            for i in stages[t]:
                take_minus(i)

        @pl.when(r == 2)
        def _():
            for i in stages[t]:
                relay(i)

        @pl.when(r == 3)
        def _():
            for i in early[t]:
                take_minus(i)
            for i in stages[t]:
                take_plus(i)

        for i in stages[t]:
            sib_wait(i)

    tokens_stage(0)
    remote(w.at[1 - h], w.at[1 - h], w_s, w_r, partner).wait_recv()

    def xq(q, tb):
        return jnp.concatenate([x[2 * q, tb], x[2 * q + 1, tb]], axis=1)

    def partial(tb, lo, hi):
        a = slice(lo * rows, hi * rows)
        return dot_nt(w[0, a, :], xq(0, tb)) + dot_nt(w[1, a, :], xq(1, tb))

    def ch(i):
        return pl.ds(rows * i, rows)

    nbr = (up_y, dn_y)
    hc = CHUNKS // 2

    def rs_copy(s, d, i):
        src = rs0.at[d, ch(i - hc * d)] if s == 0 else rs.at[d, s - 1, ch(i)]
        return remote(src, rs.at[d, s, ch(i)], rs_s.at[s, d, i], rs_r.at[s, d, i], nbr[d])

    def firsts(d):
        return range(hc) if d == 0 else range(hc, CHUNKS)

    p0 = partial(block(4), 0, CHUNKS)
    for d in range(2):
        rs0[d] = p0[d * hc * rows : (d + 1) * hc * rows].astype(BF16)
        for i in firsts(d):
            rs_copy(0, d, i).start()
    for s in range(1, 4):
        tokens_stage(s)
        for d in range(2):
            part[d] = partial(block(4 - s if d == 0 else s - 4), 0, CHUNKS)
        if s == 1:
            for d in range(2):
                for i in firsts(1 - d):
                    rs[d, 0, ch(i)] = part[d, ch(i)].astype(BF16)
                    rs_copy(1, d, i).start()
        for i in range(CHUNKS):
            for d in range(2):
                if s == 1:
                    if i not in firsts(d):
                        continue
                rs_copy(s - 1, d, i).wait_recv()
                rs[d, s - 1, ch(i)] = (rs[d, s - 1, ch(i)].astype(F32) + part[d, ch(i)]).astype(BF16)
                rs_copy(s, d, i).start()
    own[...] = partial(y, 0, CHUNKS)

    def ag_copy(s, d, i):
        b = lax.rem(y + (NY - s if d == 0 else s), NY)
        sl = dg.at[b, ch(i)]
        return remote(sl, sl, ag_s.at[s, d, i], ag_r.at[s, d, i], nbr[d])

    def ag_wait(s, d, i):
        b = lax.rem(y + (NY - 1 - s if d == 0 else s + 1), NY)
        sl = dg.at[b, ch(i)]
        remote(sl, sl, ag_s.at[s, d, i], ag_r.at[s, d, i], nbr[d]).wait_recv()

    for i in range(CHUNKS):
        for d in range(2):
            rs_copy(3, d, i).wait_recv()
        tot = own[ch(i)] + rs[0, 3, ch(i)].astype(F32) + rs[1, 3, ch(i)].astype(F32)
        gate, up = tot[:half], tot[half:]
        f = pl.ds(half * i, half)
        sg = jax.nn.sigmoid(gate)
        act = gate * sg
        hid_ref[f, :] = (act * up).astype(BF16)
        gin = dh_ref[f, :].astype(F32)
        dgate = (gin * up * sg * (1.0 + gate * (1.0 - sg))).astype(BF16)
        dup = (gin * act).astype(BF16)
        dg[y, pl.ds(rows * i, half), :] = dgate
        dg[y, pl.ds(rows * i + half, half), :] = dup
        for d in range(2):
            ag_copy(0, d, i).start()

    for q in range(2):
        wt[q] = jnp.transpose(w[q])

    def grads_of(blocks, first):
        a = jnp.concatenate([dg[b] for b in blocks], axis=1) if len(blocks) > 1 else dg[blocks[0]]
        for j in range(4):
            xs = [x[j, b] for b in blocks]
            bb = jnp.concatenate(xs, axis=0) if len(blocks) > 1 else xs[0]
            v = dot_nn(a, bb)
            col = slice(128 * (j % 2), 128 * (j % 2) + 128)
            if first:
                acc[j // 2, :, col] = v
            else:
                acc[j // 2, :, col] = acc[j // 2, :, col] + v

    def sib_copy(q, b, k):
        return remote(
            dp.at[2 * q + other, b], sib.at[q, k], sb_s.at[q, k], sb_r.at[q, k], sibling
        )

    def inputs_of(b, k):
        for q in range(2):
            v = dot_nn(wt[q], dg[b]).astype(BF16)
            dp[2 * q, b] = v[:128]
            dp[2 * q + 1, b] = v[128:]
            sib_copy(q, b, k).start()

    seq = [block(d) for d in (0, -1, 1, -2, 2, -3, 3, 4)]
    groups = ((0,), (1, 2), (3, 4), (5, 6), (7,))
    par = lax.rem(y, 2)

    z_to = (dn_z, up_z, dn_z2, up_z2)

    def z_copy(q, w_, k):
        return remote(zsum.at[q, k], zin.at[w_, k], zo_s.at[w_, k], zo_r.at[w_, k], z_to[w_])

    def z_add(q, ways, k):
        v = zsum[q, k].astype(F32)
        for w_ in ways:
            z_copy(q, w_, k).wait_recv()
            v = v + zin[w_, k].astype(F32)
        zsum[q, k] = v.astype(BF16)

    def dt_copy(k):
        return remote(
            zsum.at[qo, k], dtin.at[xl], dt_s.at[k], dt_r.at[xl], dev(z, par, c, h, seq[k])
        )

    def cores(g):
        for k in groups[g]:
            for q in range(2):
                sib_copy(q, seq[k], k).wait_recv()
                v = dp[2 * q + c, seq[k]].astype(F32) + sib[q, k].astype(F32)
                zsum[q, k] = v.astype(BF16)

            @pl.when(lax.rem(r, 2) == 1)
            def _():
                z_copy(qp, 0, k).start()
                z_copy(qm, 1, k).start()

            @pl.when(r == 0)
            def _():
                z_copy(qp, 2, k).start()

    def middle(g):
        @pl.when(r == 2)
        def _():
            for k in groups[g]:
                z_add(qp, (0, 2), k)
                z_copy(qp, 2, k).start()
                z_add(qm, (1,), k)
                z_copy(qm, 3, k).start()

    def collect(g):
        @pl.when(r == 0)
        def _():
            for k in groups[g]:
                z_add(qo, (0, 1, 2, 3), k)
                if k > 0:
                    dt_copy(k).start()
                else:

                    @pl.when(xl == par)
                    def _():
                        pltpu.make_async_copy(zsum.at[qo, 0], dtin.at[xl], dt_r.at[xl]).start()

                    @pl.when(xl != par)
                    def _():
                        dt_copy(0).start()

    inputs_of(seq[0], 0)
    grads_of([seq[0]], True)
    for s in range(1, 5):
        for i in range(CHUNKS):
            for d in range(2):
                if s < 4 or i in firsts(d):
                    ag_wait(s - 1, d, i)
                if s < 3 or (s == 3 and i in firsts(d)):
                    ag_copy(s, d, i).start()
        for k in groups[s]:
            inputs_of(seq[k], k)
        grads_of([seq[k] for k in groups[s]], False)
        if s == 4:
            gsend[...] = acc[1 - h].astype(BF16)
            gcopy = remote(gsend, grecv, g_s, g_r, partner)
            gcopy.start()
        cores(s - 1)
        if s > 1:
            middle(s - 2)
        if s > 2:
            collect(s - 3)
    cores(4)
    middle(3)
    collect(2)
    middle(4)
    collect(3)
    collect(4)

    remote(gsend, grecv, g_s, g_r, partner).wait_recv()
    for i in range(CHUNKS):
        for k in range(2):
            a = pl.ds(rows * i + half * k, half)
            grad_ref[k, pl.ds(half * i, half), :] = (
                acc[h, a, :] + grecv[a, :].astype(F32)
            ) * factor

    for s in range(2):
        remote(zsum.at[0, 0], dtin.at[s], dt_s.at[0], dt_r.at[s], sibling).wait_recv()
    tot = dtin[0].astype(F32) + dtin[1].astype(F32)
    dtok_ref[...] = jnp.transpose(tot).astype(BF16)

    wcopy.wait_send()
    xg1.wait_send()

    @pl.when(jnp.logical_not(selfcol))
    def _():
        xg0.wait_send()

    for i in range(NY):
        for q in range(2):
            cp_sib(q, i).wait_send()

    @pl.when(lax.rem(r, 2) == 0)
    def _():
        for i in range(NY):
            cp_plus(0, i, 0).wait_send()
            cp_plus(0, i, 1).wait_send()
            cp_minus(0, i, 0).wait_send()

    @pl.when(r == 0)
    def _():
        for i in range(NY):
            cp_minus(0, i, 1).wait_send()

    for s in range(4):
        for d in range(2):
            for i in range(CHUNKS):
                if s > 0 or i in firsts(d):
                    rs_copy(s, d, i).wait_send()
                if s < 3 or i in firsts(d):
                    ag_copy(s, d, i).wait_send()
    for k in range(NY):
        for q in range(2):
            sib_copy(q, seq[k], k).wait_send()

    @pl.when(lax.rem(r, 2) == 1)
    def _():
        for k in range(NY):
            z_copy(0, 0, k).wait_send()
            z_copy(0, 1, k).wait_send()

    @pl.when(lax.rem(r, 2) == 0)
    def _():
        for k in range(NY):
            z_copy(0, 2, k).wait_send()

    @pl.when(r == 2)
    def _():
        for k in range(NY):
            z_copy(0, 3, k).wait_send()

    @pl.when(r == 0)
    def _():
        for k in range(1, NY):
            dt_copy(k).wait_send()

    @pl.when(jnp.logical_and(r == 0, xl != par))
    def _():
        dt_copy(0).wait_send()

    gcopy.wait_send()


def write_out(a_ref, b_ref, c_ref, ao_ref, bo_ref, co_ref, sem):
    copies = [
        pltpu.make_async_copy(src, dst, sem.at[i])
        for i, (src, dst) in enumerate(((c_ref, co_ref), (a_ref, ao_ref), (b_ref, bo_ref)))
    ]
    for copy in copies:
        copy.start()
    for copy in copies:
        copy.wait()


def body(tokens, codes, scales, d_hidden):
    t, dloc = tokens.shape
    _, wrows, group = codes.shape
    all2 = 2 * group
    codes_t = jnp.transpose(codes, (0, 2, 1))
    dh_t = jnp.transpose(d_hidden)
    dma = pltpu.SemaphoreType.DMA
    vm = pl.BlockSpec(memory_space=pltpu.VMEM)
    hid_t, dtok, grad_t = pl.pallas_call(
        kernel,
        out_shape=(
            jax.ShapeDtypeStruct((group, t), BF16),
            jax.ShapeDtypeStruct((t, dloc), BF16),
            jax.ShapeDtypeStruct((2, group, wrows), F32),
        ),
        in_specs=[pl.BlockSpec(memory_space=pltpu.HBM)] * 4,
        out_specs=(vm, vm, vm),
        scratch_shapes=[
            pltpu.VMEM((2, group, wrows), BF16),
            pltpu.VMEM(scales.shape, BF16),
            pltpu.VMEM((group, t), BF16),
            pltpu.SemaphoreType.DMA((4,)),
            pltpu.VMEM((t, dloc), BF16),
            pltpu.VMEM((4, NY, t, dloc), BF16),
            pltpu.VMEM((2, all2, wrows), BF16),
            pltpu.VMEM((2, wrows, all2), BF16),
            pltpu.VMEM((2, all2 // 2, t), BF16),
            pltpu.VMEM((2, 4, all2, t), BF16),
            pltpu.VMEM((2, all2, t), F32),
            pltpu.VMEM((all2, t), F32),
            pltpu.VMEM((NY, all2, t), BF16),
            pltpu.VMEM((2, all2, wrows), F32),
            pltpu.VMEM((4, NY, dloc, t), BF16),
            pltpu.VMEM((2, NY, dloc, t), BF16),
            pltpu.VMEM((4, NY, dloc, t), BF16),
            pltpu.VMEM((2, NY, dloc, t), BF16),
            pltpu.VMEM((2, dloc, t), BF16),
            pltpu.VMEM((all2, wrows), BF16),
            pltpu.VMEM((all2, wrows), BF16),
            dma(()),
            dma(()),
            dma(()),
            dma((2,)),
            dma((NY,)),
            dma((2, NY)),
            dma((NY,)),
            dma((2, NY)),
            dma((NY,)),
            dma((2, NY)),
            dma((2, NY)),
            dma((4, 2, CHUNKS)),
            dma((4, 2, CHUNKS)),
            dma((4, 2, CHUNKS)),
            dma((4, 2, CHUNKS)),
            dma((2, NY)),
            dma((2, NY)),
            dma((4, NY)),
            dma((4, NY)),
            dma((NY,)),
            dma((2,)),
            dma(()),
            dma(()),
        ],
        compiler_params=pltpu.CompilerParams(collective_id=0, has_side_effects=True, vmem_limit_bytes=24 * 1024 * 1024),
    )(*(pltpu.with_memory_space_constraint(a, pltpu.HBM) for a in (tokens, codes_t, scales, dh_t)))
    hid_t, dtok, grad_t = pl.pallas_call(
        write_out,
        out_shape=tuple(jax.ShapeDtypeStruct(a.shape, a.dtype) for a in (hid_t, dtok, grad_t)),
        in_specs=[vm] * 3,
        out_specs=(pl.BlockSpec(memory_space=pltpu.HBM),) * 3,
        scratch_shapes=[dma((3,))],
        compiler_params=pltpu.CompilerParams(vmem_limit_bytes=4 * 1024 * 1024),
    )(hid_t, dtok, grad_t)
    return (jnp.transpose(hid_t), dtok, jnp.transpose(grad_t, (0, 2, 1)))


def solution(mesh):
    return jax.shard_map(
        body,
        mesh=mesh,
        in_specs=(
            P("local", "node"),
            P(None, "local", "node"),
            P(None, "local", "node"),
            P("local", "node"),
        ),
        out_specs=(P("local", "node"), P("local", "node"), P(None, "local", "node")),
        check_vma=False,
    )
```

```python
import math

import jax
import jax.numpy as jnp
from jax import lax
from jax.experimental import pallas as pl
from jax.experimental.pallas import tpu as pltpu
from jax.sharding import PartitionSpec as P

MESH = pl.DeviceIdType.MESH
BLOCK = 128
NY = 8
NZ = 8
CHUNKS = 4
F32 = jnp.float32
BF16 = jnp.bfloat16


def dot_nn(a, b):
    return lax.dot_general(a, b, (((1,), (0,)), ((), ())), preferred_element_type=F32)


def dot_nt(a, b):
    return lax.dot_general(a, b, (((1,), (1,)), ((), ())), preferred_element_type=F32)


def kernel(
    tok_hbm,
    codes_hbm,
    scale_hbm,
    dh_hbm,
    hid_ref,
    dtok_ref,
    grad_ref,
    codes_ref,
    scale_ref,
    dh_ref,
    in_sem,
    xin,
    x,
    w,
    wt,
    rs0,
    rs,
    part,
    own,
    dg,
    acc,
    dp,
    sib,
    zin,
    zsum,
    dtin,
    gsend,
    grecv,
    loc_sem,
    w_s,
    w_r,
    xg_s,
    xg_r,
    xp_s,
    xp_r,
    xm_s,
    xm_r,
    xs_s,
    xs_r,
    rs_s,
    rs_r,
    ag_s,
    ag_r,
    sb_s,
    sb_r,
    zo_s,
    zo_r,
    dt_s,
    dt_r,
    g_s,
    g_r,
):
    loads = [
        pltpu.make_async_copy(a, b, in_sem.at[i])
        for i, (a, b) in enumerate(
            ((tok_hbm, xin), (scale_hbm, scale_ref), (codes_hbm, codes_ref), (dh_hbm, dh_ref))
        )
    ]
    for load in loads:
        load.start()

    n = lax.axis_index("node")
    l = lax.axis_index("local")
    z = lax.div(n, 4)
    xl = lax.rem(lax.div(n, 2), 2)
    c = lax.rem(n, 2)
    h = lax.div(l, NY)
    y = lax.rem(l, NY)
    half = codes_ref.shape[1] // CHUNKS
    factor = 1.0 / math.sqrt(tok_hbm.shape[0] * 16)
    rows = 2 * half

    def dev(z_, xl_, c_, h_, y_):
        return (z_ * 4 + xl_ * 2 + c_, h_ * NY + y_)

    zu = lax.rem(z + 1, NZ)
    zd = lax.rem(z + NZ - 1, NZ)
    yu = lax.rem(y + 1, NY)
    yd = lax.rem(y + NY - 1, NY)
    zu2 = lax.rem(z + 2, NZ)
    zd2 = lax.rem(z + NZ - 2, NZ)
    up_z = dev(zu, xl, c, h, y)
    up_z2 = dev(zu2, xl, c, h, y)
    dn_z2 = dev(zd2, xl, c, h, y)
    dn_z = dev(zd, xl, c, h, y)
    up_y = dev(z, xl, c, h, yu)
    dn_y = dev(z, xl, c, h, yd)
    sibling = dev(z, xl, 1 - c, h, y)
    partner = dev(z, xl, c, 1 - h, y)
    other = 1 - c

    barrier = pltpu.get_barrier_semaphore()
    peers = [up_z, dn_z, up_z2, dn_z2, sibling, partner]
    for dx in range(2):
        for dy in range(NY):
            if dx or dy:
                peers.append(dev(z, lax.rem(xl + dx, 2), c, h, lax.rem(y + dy, NY)))
    for peer in peers:
        pl.semaphore_signal(barrier, inc=1, device_id=peer, device_id_type=MESH)

    def remote(src, dst, ss, rr, to):
        return pltpu.make_async_remote_copy(
            src_ref=src, dst_ref=dst, send_sem=ss, recv_sem=rr, device_id=to, device_id_type=MESH
        )

    loads[0].wait()
    loads[3].wait()

    pl.semaphore_wait(barrier, len(peers))

    ystar = 2 * lax.rem(z, 4) + xl
    qsrc = lax.div(z, 4)
    myslot = x.at[2 * qsrc + c, y]
    own_col = dev(z, xl, c, h, ystar)
    oth_col = dev(z, 1 - xl, c, h, ystar)
    xg0 = remote(xin, myslot, xg_s.at[0], xg_r.at[y], own_col)
    xg1 = remote(xin, myslot, xg_s.at[1], xg_r.at[y], oth_col)
    xg1.start()
    selfcol = ystar == y

    @pl.when(selfcol)
    def _():
        pltpu.make_async_copy(xin, myslot, xg_r.at[y]).start()

    @pl.when(jnp.logical_not(selfcol))
    def _():
        xg0.start()

    loads[1].wait()
    loads[2].wait()
    pick = (
        lax.broadcasted_iota(jnp.int32, (2, 2 * BLOCK), 1) // BLOCK
        == lax.broadcasted_iota(jnp.int32, (2, 2 * BLOCK), 0)
    ).astype(BF16)
    for k in range(2):
        spread = lax.dot_general(
            scale_ref[k],
            pick,
            (((0,), (0,)), ((), ())),
            preferred_element_type=F32,
        )
        for i in range(CHUNKS):
            f = pl.ds(half * i, half)
            code = codes_ref[k, f, :].astype(F32)
            s = spread[half * i : half * (i + 1)]
            w[h, pl.ds(rows * i + half * k, half), :] = (code * s).astype(BF16)
    wcopy = remote(w.at[h], w.at[h], w_s, w_r, partner)
    wcopy.start()

    dz = lax.rem(z - lax.div(y, 2) + NZ, NZ)
    r = lax.rem(dz, 4)
    qo = lax.div(dz, 4)
    qp = lax.div(lax.rem(dz + 7, NZ), 4)
    qm = 1 - qp

    def block(d):
        return lax.rem(y + d + NY, NY)

    order = [block(d) for d in (4, 3, -3, 2, -2, 1, -1, 0)]

    def slot(q, tb):
        return x.at[2 * q + c, tb]

    def cp_plus(q, i, far):
        s = slot(q, order[i])
        return remote(s, s, xp_s.at[far, i], xp_r.at[i], up_z2 if far else up_z)

    def cp_minus(q, i, far):
        s = slot(q, order[i])
        return remote(s, s, xm_s.at[far, i], xm_r.at[i], dn_z2 if far else dn_z)

    def cp_sib(q, i):
        s = slot(q, order[i])
        return remote(s, s, xs_s.at[q, i], xs_r.at[q, i], sibling)

    def sib_wait(i):
        for q in range(2):
            s = x.at[2 * q + other, order[i]]
            remote(s, s, xs_s.at[q, i], xs_r.at[q, i], sibling).wait_recv()

    def spread_own(i):
        remote(xin, slot(qo, order[i]), xg_s.at[0], xg_r.at[order[i]], own_col).wait_recv()
        for far in (1, 0):
            cp_plus(qo, i, far).start()
            cp_minus(qo, i, far).start()
        cp_sib(qo, i).start()

    def take_plus(i):
        cp_plus(qp, i, 0).wait_recv()
        cp_sib(qp, i).start()

    def take_minus(i):
        cp_minus(qm, i, 0).wait_recv()
        cp_sib(qm, i).start()

    def relay(i):
        cp_plus(qp, i, 0).wait_recv()
        cp_plus(qp, i, 1).start()
        cp_plus(qp, i, 0).start()
        cp_sib(qp, i).start()
        cp_minus(qm, i, 0).wait_recv()
        cp_minus(qm, i, 0).start()
        cp_sib(qm, i).start()

    stages = ((0,), (1, 2), (3, 4), (5, 6, 7))
    early = ((0, 1, 2), (3, 4), (5, 6), (7,))
    ahead = ((0, 1, 2), (3,), (), ())

    def tokens_stage(t):
        @pl.when(r == 0)
        def _():
            if t == 0:
                for i in range(NY):
                    spread_own(i)
            for i in stages[t]:
                take_plus(i)

        @pl.when(r == 1)
        def _():
            for i in early[t]:
                take_plus(i)
            for i in stages[t]:
                take_minus(i)

        @pl.when(r == 2)
        def _():
            for i in ahead[t]:
                relay(i)

        @pl.when(r == 3)
        def _():
            for i in early[t]:
                take_minus(i)
            for i in stages[t]:
                take_plus(i)

        for i in stages[t]:
            sib_wait(i)

    tokens_stage(0)
    remote(w.at[1 - h], w.at[1 - h], w_s, w_r, partner).wait_recv()

    def xq(q, tb):
        return jnp.concatenate([x[2 * q, tb], x[2 * q + 1, tb]], axis=1)

    def partial(tb, lo, hi):
        a = slice(lo * rows, hi * rows)
        return dot_nt(w[0, a, :], xq(0, tb)) + dot_nt(w[1, a, :], xq(1, tb))

    def ch(i):
        return pl.ds(rows * i, rows)

    nbr = (up_y, dn_y)
    hc = CHUNKS // 2

    def rs_copy(s, d, i):
        src = rs0.at[d, ch(i - hc * d)] if s == 0 else rs.at[d, s - 1, ch(i)]
        return remote(src, rs.at[d, s, ch(i)], rs_s.at[s, d, i], rs_r.at[s, d, i], nbr[d])

    def firsts(d):
        return range(hc) if d == 0 else range(hc, CHUNKS)

    p0 = partial(block(4), 0, CHUNKS)
    for d in range(2):
        rs0[d] = p0[d * hc * rows : (d + 1) * hc * rows].astype(BF16)
        for i in firsts(d):
            rs_copy(0, d, i).start()
    for s in range(1, 4):
        tokens_stage(s)
        for d in range(2):
            part[d] = partial(block(4 - s if d == 0 else s - 4), 0, CHUNKS)
        if s == 1:
            for d in range(2):
                for i in firsts(1 - d):
                    rs[d, 0, ch(i)] = part[d, ch(i)].astype(BF16)
                    rs_copy(1, d, i).start()
        for i in range(CHUNKS):
            for d in range(2):
                if s == 1:
                    if i not in firsts(d):
                        continue
                rs_copy(s - 1, d, i).wait_recv()
                rs[d, s - 1, ch(i)] = (rs[d, s - 1, ch(i)].astype(F32) + part[d, ch(i)]).astype(BF16)
                rs_copy(s, d, i).start()
            nxt = {(1, 0): 4, (1, 2): 5, (2, 0): 6, (2, 2): 7}.get((s, i))
            if nxt is not None:

                @pl.when(r == 2)
                def _():
                    relay(nxt)

    own[...] = partial(y, 0, CHUNKS)

    def ag_copy(s, d, i):
        b = lax.rem(y + (NY - s if d == 0 else s), NY)
        sl = dg.at[b, ch(i)]
        return remote(sl, sl, ag_s.at[s, d, i], ag_r.at[s, d, i], nbr[d])

    def ag_wait(s, d, i):
        b = lax.rem(y + (NY - 1 - s if d == 0 else s + 1), NY)
        sl = dg.at[b, ch(i)]
        remote(sl, sl, ag_s.at[s, d, i], ag_r.at[s, d, i], nbr[d]).wait_recv()

    for i in range(CHUNKS):
        for d in range(2):
            rs_copy(3, d, i).wait_recv()
        tot = own[ch(i)] + rs[0, 3, ch(i)].astype(F32) + rs[1, 3, ch(i)].astype(F32)
        gate, up = tot[:half], tot[half:]
        f = pl.ds(half * i, half)
        sg = jax.nn.sigmoid(gate)
        act = gate * sg
        hid_ref[f, :] = (act * up).astype(BF16)
        gin = dh_ref[f, :].astype(F32)
        dgate = (gin * up * sg * (1.0 + gate * (1.0 - sg))).astype(BF16)
        dup = (gin * act).astype(BF16)
        dg[y, pl.ds(rows * i, half), :] = dgate
        dg[y, pl.ds(rows * i + half, half), :] = dup
        for d in range(2):
            ag_copy(0, d, i).start()

    for q in range(2):
        wt[q] = jnp.transpose(w[q])

    def grads_of(blocks, first):
        a = jnp.concatenate([dg[b] for b in blocks], axis=1) if len(blocks) > 1 else dg[blocks[0]]
        for j in range(4):
            xs = [x[j, b] for b in blocks]
            bb = jnp.concatenate(xs, axis=0) if len(blocks) > 1 else xs[0]
            v = dot_nn(a, bb)
            col = slice(128 * (j % 2), 128 * (j % 2) + 128)
            if first:
                acc[j // 2, :, col] = v
            else:
                acc[j // 2, :, col] = acc[j // 2, :, col] + v

    def sib_copy(q, b, k):
        return remote(
            dp.at[2 * q + other, b], sib.at[q, k], sb_s.at[q, k], sb_r.at[q, k], sibling
        )

    def inputs_of(b, k):
        for q in range(2):
            v = dot_nn(wt[q], dg[b]).astype(BF16)
            dp[2 * q, b] = v[:128]
            dp[2 * q + 1, b] = v[128:]
            sib_copy(q, b, k).start()

    seq = [block(d) for d in (0, -1, 1, -2, 2, -3, 3, 4)]
    groups = ((0,), (1, 2), (3, 4), (5, 6), (7,))
    par = lax.rem(y, 2)

    z_to = (dn_z, up_z, dn_z2, up_z2)

    def z_copy(q, w_, k):
        return remote(zsum.at[q, k], zin.at[w_, k], zo_s.at[w_, k], zo_r.at[w_, k], z_to[w_])

    def z_add(q, ways, k):
        v = zsum[q, k].astype(F32)
        for w_ in ways:
            z_copy(q, w_, k).wait_recv()
            v = v + zin[w_, k].astype(F32)
        zsum[q, k] = v.astype(BF16)

    def dt_copy(k):
        return remote(
            zsum.at[qo, k], dtin.at[xl], dt_s.at[k], dt_r.at[xl], dev(z, par, c, h, seq[k])
        )

    def cores(g):
        for k in groups[g]:
            for q in range(2):
                sib_copy(q, seq[k], k).wait_recv()
                v = dp[2 * q + c, seq[k]].astype(F32) + sib[q, k].astype(F32)
                zsum[q, k] = v.astype(BF16)

            @pl.when(lax.rem(r, 2) == 1)
            def _():
                z_copy(qp, 0, k).start()
                z_copy(qm, 1, k).start()

            @pl.when(r == 0)
            def _():
                z_copy(qp, 2, k).start()

    def middle(g):
        @pl.when(r == 2)
        def _():
            for k in groups[g]:
                z_add(qp, (0, 2), k)
                z_copy(qp, 2, k).start()
                z_add(qm, (1,), k)
                z_copy(qm, 3, k).start()

    def collect(g):
        @pl.when(r == 0)
        def _():
            for k in groups[g]:
                z_add(qo, (0, 1, 2, 3), k)
                if k > 0:
                    dt_copy(k).start()
                else:

                    @pl.when(xl == par)
                    def _():
                        pltpu.make_async_copy(zsum.at[qo, 0], dtin.at[xl], dt_r.at[xl]).start()

                    @pl.when(xl != par)
                    def _():
                        dt_copy(0).start()

    inputs_of(seq[0], 0)
    grads_of([seq[0]], True)
    for s in range(1, 5):
        for i in range(CHUNKS):
            for d in range(2):
                if s < 4 or i in firsts(d):
                    ag_wait(s - 1, d, i)
                if s < 3 or (s == 3 and i in firsts(d)):
                    ag_copy(s, d, i).start()
        for k in groups[s]:
            inputs_of(seq[k], k)
        grads_of([seq[k] for k in groups[s]], False)
        if s == 4:
            gsend[...] = acc[1 - h].astype(BF16)
            gcopy = remote(gsend, grecv, g_s, g_r, partner)
            gcopy.start()
        cores(s - 1)
        if s > 1:
            middle(s - 2)
        if s > 2:
            collect(s - 3)
    cores(4)
    middle(3)
    collect(2)
    middle(4)
    collect(3)
    collect(4)

    remote(gsend, grecv, g_s, g_r, partner).wait_recv()
    for i in range(CHUNKS):
        for k in range(2):
            a = pl.ds(rows * i + half * k, half)
            grad_ref[k, pl.ds(half * i, half), :] = (
                acc[h, a, :] + grecv[a, :].astype(F32)
            ) * factor

    for s in range(2):
        remote(zsum.at[0, 0], dtin.at[s], dt_s.at[0], dt_r.at[s], sibling).wait_recv()
    tot = dtin[0].astype(F32) + dtin[1].astype(F32)
    dtok_ref[...] = jnp.transpose(tot).astype(BF16)

    wcopy.wait_send()
    xg1.wait_send()

    @pl.when(jnp.logical_not(selfcol))
    def _():
        xg0.wait_send()

    for i in range(NY):
        for q in range(2):
            cp_sib(q, i).wait_send()

    @pl.when(lax.rem(r, 2) == 0)
    def _():
        for i in range(NY):
            cp_plus(0, i, 0).wait_send()
            cp_plus(0, i, 1).wait_send()
            cp_minus(0, i, 0).wait_send()

    @pl.when(r == 0)
    def _():
        for i in range(NY):
            cp_minus(0, i, 1).wait_send()

    for s in range(4):
        for d in range(2):
            for i in range(CHUNKS):
                if s > 0 or i in firsts(d):
                    rs_copy(s, d, i).wait_send()
                if s < 3 or i in firsts(d):
                    ag_copy(s, d, i).wait_send()
    for k in range(NY):
        for q in range(2):
            sib_copy(q, seq[k], k).wait_send()

    @pl.when(lax.rem(r, 2) == 1)
    def _():
        for k in range(NY):
            z_copy(0, 0, k).wait_send()
            z_copy(0, 1, k).wait_send()

    @pl.when(lax.rem(r, 2) == 0)
    def _():
        for k in range(NY):
            z_copy(0, 2, k).wait_send()

    @pl.when(r == 2)
    def _():
        for k in range(NY):
            z_copy(0, 3, k).wait_send()

    @pl.when(r == 0)
    def _():
        for k in range(1, NY):
            dt_copy(k).wait_send()

    @pl.when(jnp.logical_and(r == 0, xl != par))
    def _():
        dt_copy(0).wait_send()

    gcopy.wait_send()


def write_out(a_ref, b_ref, c_ref, ao_ref, bo_ref, co_ref, sem):
    copies = [
        pltpu.make_async_copy(src, dst, sem.at[i])
        for i, (src, dst) in enumerate(((c_ref, co_ref), (a_ref, ao_ref), (b_ref, bo_ref)))
    ]
    for copy in copies:
        copy.start()
    for copy in copies:
        copy.wait()


def body(tokens, codes, scales, d_hidden):
    t, dloc = tokens.shape
    _, wrows, group = codes.shape
    all2 = 2 * group
    codes_t = jnp.transpose(codes, (0, 2, 1))
    dh_t = jnp.transpose(d_hidden)
    dma = pltpu.SemaphoreType.DMA
    vm = pl.BlockSpec(memory_space=pltpu.VMEM)
    hid_t, dtok, grad_t = pl.pallas_call(
        kernel,
        out_shape=(
            jax.ShapeDtypeStruct((group, t), BF16),
            jax.ShapeDtypeStruct((t, dloc), BF16),
            jax.ShapeDtypeStruct((2, group, wrows), F32),
        ),
        in_specs=[pl.BlockSpec(memory_space=pltpu.HBM)] * 4,
        out_specs=(vm, vm, vm),
        scratch_shapes=[
            pltpu.VMEM((2, group, wrows), BF16),
            pltpu.VMEM(scales.shape, BF16),
            pltpu.VMEM((group, t), BF16),
            pltpu.SemaphoreType.DMA((4,)),
            pltpu.VMEM((t, dloc), BF16),
            pltpu.VMEM((4, NY, t, dloc), BF16),
            pltpu.VMEM((2, all2, wrows), BF16),
            pltpu.VMEM((2, wrows, all2), BF16),
            pltpu.VMEM((2, all2 // 2, t), BF16),
            pltpu.VMEM((2, 4, all2, t), BF16),
            pltpu.VMEM((2, all2, t), F32),
            pltpu.VMEM((all2, t), F32),
            pltpu.VMEM((NY, all2, t), BF16),
            pltpu.VMEM((2, all2, wrows), F32),
            pltpu.VMEM((4, NY, dloc, t), BF16),
            pltpu.VMEM((2, NY, dloc, t), BF16),
            pltpu.VMEM((4, NY, dloc, t), BF16),
            pltpu.VMEM((2, NY, dloc, t), BF16),
            pltpu.VMEM((2, dloc, t), BF16),
            pltpu.VMEM((all2, wrows), BF16),
            pltpu.VMEM((all2, wrows), BF16),
            dma(()),
            dma(()),
            dma(()),
            dma((2,)),
            dma((NY,)),
            dma((2, NY)),
            dma((NY,)),
            dma((2, NY)),
            dma((NY,)),
            dma((2, NY)),
            dma((2, NY)),
            dma((4, 2, CHUNKS)),
            dma((4, 2, CHUNKS)),
            dma((4, 2, CHUNKS)),
            dma((4, 2, CHUNKS)),
            dma((2, NY)),
            dma((2, NY)),
            dma((4, NY)),
            dma((4, NY)),
            dma((NY,)),
            dma((2,)),
            dma(()),
            dma(()),
        ],
        compiler_params=pltpu.CompilerParams(collective_id=0, has_side_effects=True, vmem_limit_bytes=24 * 1024 * 1024),
    )(*(pltpu.with_memory_space_constraint(a, pltpu.HBM) for a in (tokens, codes_t, scales, dh_t)))
    hid_t, dtok, grad_t = pl.pallas_call(
        write_out,
        out_shape=tuple(jax.ShapeDtypeStruct(a.shape, a.dtype) for a in (hid_t, dtok, grad_t)),
        in_specs=[vm] * 3,
        out_specs=(pl.BlockSpec(memory_space=pltpu.HBM),) * 3,
        scratch_shapes=[dma((3,))],
        compiler_params=pltpu.CompilerParams(vmem_limit_bytes=4 * 1024 * 1024),
    )(hid_t, dtok, grad_t)
    return (jnp.transpose(hid_t), dtok, jnp.transpose(grad_t, (0, 2, 1)))


def solution(mesh):
    return jax.shard_map(
        body,
        mesh=mesh,
        in_specs=(
            P("local", "node"),
            P(None, "local", "node"),
            P(None, "local", "node"),
            P("local", "node"),
        ),
        out_specs=(P("local", "node"), P("local", "node"), P(None, "local", "node")),
        check_vma=False,
    )
```

```python
import math

import jax
import jax.numpy as jnp
from jax import lax
from jax.experimental import pallas as pl
from jax.experimental.pallas import tpu as pltpu
from jax.sharding import PartitionSpec as P

MESH = pl.DeviceIdType.MESH
BLOCK = 128
NY = 8
NZ = 8
CHUNKS = 4
F32 = jnp.float32
BF16 = jnp.bfloat16


def dot_nn(a, b):
    return lax.dot_general(a, b, (((1,), (0,)), ((), ())), preferred_element_type=F32)


def dot_nt(a, b):
    return lax.dot_general(a, b, (((1,), (1,)), ((), ())), preferred_element_type=F32)


def kernel(
    tok_hbm,
    codes_hbm,
    scale_hbm,
    dh_hbm,
    hid_ref,
    dtok_ref,
    grad_ref,
    codes_ref,
    scale_ref,
    dh_ref,
    in_sem,
    xin,
    x,
    w,
    wt,
    rs0,
    rs,
    part,
    own,
    dg,
    acc,
    dp,
    sib,
    zin,
    zx,
    zsum,
    dtin,
    gsend,
    grecv,
    loc_sem,
    w_s,
    w_r,
    xg_s,
    xg_r,
    xp_s,
    xp_r,
    xm_s,
    xm_r,
    xs_s,
    xs_r,
    rs_s,
    rs_r,
    ag_s,
    ag_r,
    sb_s,
    sb_r,
    zo_s,
    zo_r,
    zx_s,
    zx_r,
    dt_s,
    dt_r,
    g_s,
    g_r,
):
    loads = [
        pltpu.make_async_copy(a, b, in_sem.at[i])
        for i, (a, b) in enumerate(
            ((tok_hbm, xin), (scale_hbm, scale_ref), (codes_hbm, codes_ref), (dh_hbm, dh_ref))
        )
    ]
    for load in loads:
        load.start()

    n = lax.axis_index("node")
    l = lax.axis_index("local")
    z = lax.div(n, 4)
    xl = lax.rem(lax.div(n, 2), 2)
    c = lax.rem(n, 2)
    h = lax.div(l, NY)
    y = lax.rem(l, NY)
    half = codes_ref.shape[1] // CHUNKS
    factor = 1.0 / math.sqrt(tok_hbm.shape[0] * 16)
    rows = 2 * half

    def dev(z_, xl_, c_, h_, y_):
        return (z_ * 4 + xl_ * 2 + c_, h_ * NY + y_)

    zu = lax.rem(z + 1, NZ)
    zd = lax.rem(z + NZ - 1, NZ)
    yu = lax.rem(y + 1, NY)
    yd = lax.rem(y + NY - 1, NY)
    zu2 = lax.rem(z + 2, NZ)
    zd2 = lax.rem(z + NZ - 2, NZ)
    up_z = dev(zu, xl, c, h, y)
    up_z2 = dev(zu2, xl, c, h, y)
    dn_z2 = dev(zd2, xl, c, h, y)
    dn_z = dev(zd, xl, c, h, y)
    up_y = dev(z, xl, c, h, yu)
    dn_y = dev(z, xl, c, h, yd)
    sibling = dev(z, xl, 1 - c, h, y)
    partner = dev(z, xl, c, 1 - h, y)
    other = 1 - c

    barrier = pltpu.get_barrier_semaphore()
    peers = [up_z, dn_z, up_z2, dn_z2, sibling, partner]
    cross = [dev(z_, xl, other, h, y) for z_ in (zd, zu, zd2, zu2)]
    peers += cross
    for dx in range(2):
        for dy in range(NY):
            if dx or dy:
                peers.append(dev(z, lax.rem(xl + dx, 2), c, h, lax.rem(y + dy, NY)))
    for peer in peers:
        pl.semaphore_signal(barrier, inc=1, device_id=peer, device_id_type=MESH)

    def remote(src, dst, ss, rr, to):
        return pltpu.make_async_remote_copy(
            src_ref=src, dst_ref=dst, send_sem=ss, recv_sem=rr, device_id=to, device_id_type=MESH
        )

    loads[0].wait()
    loads[3].wait()

    pl.semaphore_wait(barrier, len(peers))

    ystar = 2 * lax.rem(z, 4) + xl
    qsrc = lax.div(z, 4)
    myslot = x.at[2 * qsrc + c, y]
    own_col = dev(z, xl, c, h, ystar)
    oth_col = dev(z, 1 - xl, c, h, ystar)
    xg0 = remote(xin, myslot, xg_s.at[0], xg_r.at[y], own_col)
    xg1 = remote(xin, myslot, xg_s.at[1], xg_r.at[y], oth_col)
    xg1.start()
    selfcol = ystar == y

    @pl.when(selfcol)
    def _():
        pltpu.make_async_copy(xin, myslot, xg_r.at[y]).start()

    @pl.when(jnp.logical_not(selfcol))
    def _():
        xg0.start()

    loads[1].wait()
    loads[2].wait()
    pick = (
        lax.broadcasted_iota(jnp.int32, (2, 2 * BLOCK), 1) // BLOCK
        == lax.broadcasted_iota(jnp.int32, (2, 2 * BLOCK), 0)
    ).astype(BF16)
    for k in range(2):
        spread = lax.dot_general(
            scale_ref[k],
            pick,
            (((0,), (0,)), ((), ())),
            preferred_element_type=F32,
        )
        for i in range(CHUNKS):
            f = pl.ds(half * i, half)
            code = codes_ref[k, f, :].astype(F32)
            s = spread[half * i : half * (i + 1)]
            w[h, pl.ds(rows * i + half * k, half), :] = (code * s).astype(BF16)
    wcopy = remote(w.at[h], w.at[h], w_s, w_r, partner)
    wcopy.start()

    dz = lax.rem(z - lax.div(y, 2) + NZ, NZ)
    r = lax.rem(dz, 4)
    qo = lax.div(dz, 4)
    qp = lax.div(lax.rem(dz + 7, NZ), 4)
    qm = 1 - qp

    def block(d):
        return lax.rem(y + d + NY, NY)

    order = [block(d) for d in (4, 3, -3, 2, -2, 1, -1, 0)]

    def slot(q, tb):
        return x.at[2 * q + c, tb]

    def cp_plus(q, i, far):
        s = slot(q, order[i])
        return remote(s, s, xp_s.at[far, i], xp_r.at[i], up_z2 if far else up_z)

    def cp_minus(q, i, far):
        s = slot(q, order[i])
        return remote(s, s, xm_s.at[far, i], xm_r.at[i], dn_z2 if far else dn_z)

    def cp_sib(q, i):
        s = slot(q, order[i])
        return remote(s, s, xs_s.at[q, i], xs_r.at[q, i], sibling)

    def sib_wait(i):
        for q in range(2):
            s = x.at[2 * q + other, order[i]]
            remote(s, s, xs_s.at[q, i], xs_r.at[q, i], sibling).wait_recv()

    def spread_own(i):
        remote(xin, slot(qo, order[i]), xg_s.at[0], xg_r.at[order[i]], own_col).wait_recv()
        for far in (1, 0):
            cp_plus(qo, i, far).start()
            cp_minus(qo, i, far).start()
        cp_sib(qo, i).start()

    def take_plus(i):
        cp_plus(qp, i, 0).wait_recv()
        cp_sib(qp, i).start()

    def take_minus(i):
        cp_minus(qm, i, 0).wait_recv()
        cp_sib(qm, i).start()

    def relay(i):
        cp_plus(qp, i, 0).wait_recv()
        cp_plus(qp, i, 1).start()
        cp_plus(qp, i, 0).start()
        cp_sib(qp, i).start()
        cp_minus(qm, i, 0).wait_recv()
        cp_minus(qm, i, 0).start()
        cp_sib(qm, i).start()

    stages = ((0,), (1, 2), (3, 4), (5, 6, 7))
    early = ((0, 1, 2), (3, 4), (5, 6), (7,))
    ahead = ((0, 1, 2), (3,), (), ())

    def tokens_stage(t):
        @pl.when(r == 0)
        def _():
            if t == 0:
                for i in range(NY):
                    spread_own(i)
            for i in stages[t]:
                take_plus(i)

        @pl.when(r == 1)
        def _():
            for i in early[t]:
                take_plus(i)
            for i in stages[t]:
                take_minus(i)

        @pl.when(r == 2)
        def _():
            for i in ahead[t]:
                relay(i)

        @pl.when(r == 3)
        def _():
            for i in early[t]:
                take_minus(i)
            for i in stages[t]:
                take_plus(i)

        for i in stages[t]:
            sib_wait(i)

    tokens_stage(0)
    remote(w.at[1 - h], w.at[1 - h], w_s, w_r, partner).wait_recv()

    def xq(q, tb):
        return jnp.concatenate([x[2 * q, tb], x[2 * q + 1, tb]], axis=1)

    def partial(tb, lo, hi):
        a = slice(lo * rows, hi * rows)
        return dot_nt(w[0, a, :], xq(0, tb)) + dot_nt(w[1, a, :], xq(1, tb))

    def ch(i):
        return pl.ds(rows * i, rows)

    nbr = (up_y, dn_y)
    hc = CHUNKS // 2

    def rs_copy(s, d, i):
        src = rs0.at[d, ch(i - hc * d)] if s == 0 else rs.at[d, s - 1, ch(i)]
        return remote(src, rs.at[d, s, ch(i)], rs_s.at[s, d, i], rs_r.at[s, d, i], nbr[d])

    def firsts(d):
        return range(hc) if d == 0 else range(hc, CHUNKS)

    for d in range(2):
        rs0[d] = partial(block(4), d * hc, (d + 1) * hc).astype(BF16)
        for i in firsts(d):
            rs_copy(0, d, i).start()
    for s in range(1, 4):
        tokens_stage(s)
        for d in range(2):
            part[d] = partial(block(4 - s if d == 0 else s - 4), 0, CHUNKS)
            if s == 1:
                for i in firsts(1 - d):
                    rs[d, 0, ch(i)] = part[d, ch(i)].astype(BF16)
                    rs_copy(1, d, i).start()
        for i in range(CHUNKS):
            for d in range(2):
                if s == 1:
                    if i not in firsts(d):
                        continue
                rs_copy(s - 1, d, i).wait_recv()
                rs[d, s - 1, ch(i)] = (rs[d, s - 1, ch(i)].astype(F32) + part[d, ch(i)]).astype(BF16)
                rs_copy(s, d, i).start()
            nxt = {(1, 0): 4, (1, 2): 5, (2, 0): 6, (2, 2): 7}.get((s, i))
            if nxt is not None:

                @pl.when(r == 2)
                def _():
                    relay(nxt)

    own[...] = partial(y, 0, CHUNKS)

    def ag_copy(s, d, i):
        b = lax.rem(y + (NY - s if d == 0 else s), NY)
        sl = dg.at[b, ch(i)]
        return remote(sl, sl, ag_s.at[s, d, i], ag_r.at[s, d, i], nbr[d])

    def ag_wait(s, d, i):
        b = lax.rem(y + (NY - 1 - s if d == 0 else s + 1), NY)
        sl = dg.at[b, ch(i)]
        remote(sl, sl, ag_s.at[s, d, i], ag_r.at[s, d, i], nbr[d]).wait_recv()

    for i in range(CHUNKS):
        for d in range(2):
            rs_copy(3, d, i).wait_recv()
        tot = own[ch(i)] + rs[0, 3, ch(i)].astype(F32) + rs[1, 3, ch(i)].astype(F32)
        gate, up = tot[:half], tot[half:]
        f = pl.ds(half * i, half)
        sg = jax.nn.sigmoid(gate)
        act = gate * sg
        hid_ref[f, :] = (act * up).astype(BF16)
        gin = dh_ref[f, :].astype(F32)
        dgate = (gin * up * sg * (1.0 + gate * (1.0 - sg))).astype(BF16)
        dup = (gin * act).astype(BF16)
        dg[y, pl.ds(rows * i, half), :] = dgate
        dg[y, pl.ds(rows * i + half, half), :] = dup
        for d in range(2):
            ag_copy(0, d, i).start()

    for q in range(2):
        wt[q] = jnp.transpose(w[q])

    def grads_of(blocks, first):
        a = jnp.concatenate([dg[b] for b in blocks], axis=1) if len(blocks) > 1 else dg[blocks[0]]
        for j in range(4):
            xs = [x[j, b] for b in blocks]
            bb = jnp.concatenate(xs, axis=0) if len(blocks) > 1 else xs[0]
            v = dot_nn(a, bb)
            col = slice(128 * (j % 2), 128 * (j % 2) + 128)
            if first:
                acc[j // 2, :, col] = v
            else:
                acc[j // 2, :, col] = acc[j // 2, :, col] + v

    def sib_copy(q, b, k):
        return remote(
            dp.at[2 * q + other, b], sib.at[q, k], sb_s.at[q, k], sb_r.at[q, k], sibling
        )

    def inputs_of(b, k):
        for q in range(2):
            v = dot_nn(wt[q], dg[b]).astype(BF16)
            dp[2 * q, b] = v[:128]
            dp[2 * q + 1, b] = v[128:]
        if k == 7:
            last_leaves()
        for q in range(2):
            sib_copy(q, b, k).start()

    seq = [block(d) for d in (0, -1, 1, -2, 2, -3, 3, 4)]
    groups = ((0,), (1, 2), (3, 4), (5, 6), (7,))
    par = lax.rem(y, 2)

    z_to = (dn_z, up_z, dn_z2, up_z2)

    def z_copy(q, w_, k):
        return remote(zsum.at[q, k], zin.at[w_, k], zo_s.at[w_, k], zo_r.at[w_, k], z_to[w_])

    def z_add(q, ways, k, crossed=()):
        v = zsum[q, k].astype(F32)
        for w_ in ways:
            z_copy(q, w_, k).wait_recv()
            v = v + zin[w_, k].astype(F32)
        for w_ in crossed if k == 7 else ():
            z_cross(q, w_).wait_recv()
            v = v + zx[w_].astype(F32)
        zsum[q, k] = v.astype(BF16)

    def dt_copy(k):
        return remote(
            zsum.at[qo, k], dtin.at[xl], dt_s.at[k], dt_r.at[xl], dev(z, par, c, h, seq[k])
        )

    def z_direct(q, w_):
        return remote(
            dp.at[2 * q + c, seq[7]], zin.at[w_, 7], zo_s.at[w_, 7], zo_r.at[w_, 7], z_to[w_]
        )

    def z_cross(q, w_):
        return remote(
            dp.at[2 * q + other, seq[7]], zx.at[w_], zx_s.at[w_], zx_r.at[w_], cross[w_]
        )

    def last_leaves():
        @pl.when(lax.rem(r, 2) == 1)
        def _():
            for q, w_ in ((qp, 0), (qm, 1)):
                z_direct(q, w_).start()
                z_cross(q, w_).start()

        @pl.when(r == 0)
        def _():
            z_direct(qp, 2).start()
            z_cross(qp, 2).start()

    def cores(g):
        for k in groups[g]:
            for q in range(2):
                sib_copy(q, seq[k], k).wait_recv()
                v = dp[2 * q + c, seq[k]].astype(F32) + sib[q, k].astype(F32)
                zsum[q, k] = v.astype(BF16)

            if k == 7:
                continue

            @pl.when(lax.rem(r, 2) == 1)
            def _():
                z_copy(qp, 0, k).start()
                z_copy(qm, 1, k).start()

            @pl.when(r == 0)
            def _():
                z_copy(qp, 2, k).start()

    def middle(g):
        @pl.when(r == 2)
        def _():
            for k in groups[g]:
                z_add(qp, (0, 2), k, (0, 2))
                z_copy(qp, 2, k).start()
                z_add(qm, (1,), k, (1,))
                z_copy(qm, 3, k).start()

    def collect(g):
        @pl.when(r == 0)
        def _():
            for k in groups[g]:
                z_add(qo, (0, 1, 2, 3), k, (0, 1))
                if k > 0:
                    dt_copy(k).start()
                else:

                    @pl.when(xl == par)
                    def _():
                        pltpu.make_async_copy(zsum.at[qo, 0], dtin.at[xl], dt_r.at[xl]).start()

                    @pl.when(xl != par)
                    def _():
                        dt_copy(0).start()

    inputs_of(seq[0], 0)
    grads_of([seq[0]], True)
    def g_copy(i):
        return remote(gsend.at[ch(i)], grecv.at[ch(i)], g_s.at[i], g_r.at[i], partner)

    for s in range(1, 4):
        for i in range(CHUNKS):
            for d in range(2):
                ag_wait(s - 1, d, i)
                if s < 3 or i in firsts(d):
                    ag_copy(s, d, i).start()
            if i == 1:
                cores(s - 1)
        for k in groups[s]:
            inputs_of(seq[k], k)
        grads_of([seq[k] for k in groups[s]], False)
        middle(s - 1)
        if s > 1:
            collect(s - 2)

    def send_grads(i):
        pair = jnp.concatenate([x[2 * (1 - h) + j, seq[7]] for j in range(2)], axis=1)
        v = dot_nn(dg[seq[7], ch(i)], pair)
        gsend[ch(i)] = (acc[1 - h, ch(i)] + v).astype(BF16)
        g_copy(i).start()

    for i in range(hc):
        ag_wait(3, 0, i)
        ag_wait(3, 1, i + hc)
        if i == hc - 1:
            inputs_of(seq[7], 7)
        send_grads(i)
        send_grads(i + hc)
        if i == 0:
            cores(3)
    collect(2)
    cores(4)
    for j in range(2):
        col = slice(128 * j, 128 * j + 128)
        acc[h, :, col] = acc[h, :, col] + dot_nn(dg[seq[7]], x[2 * h + j, seq[7]])
    middle(3)
    middle(4)
    collect(3)
    collect(4)

    for i in range(CHUNKS):
        g_copy(i).wait_recv()
        for k in range(2):
            a = pl.ds(rows * i + half * k, half)
            grad_ref[k, pl.ds(half * i, half), :] = (
                acc[h, a, :] + grecv[a, :].astype(F32)
            ) * factor

    for s in range(2):
        remote(zsum.at[0, 0], dtin.at[s], dt_s.at[0], dt_r.at[s], sibling).wait_recv()
    tot = dtin[0].astype(F32) + dtin[1].astype(F32)
    dtok_ref[...] = jnp.transpose(tot).astype(BF16)

    wcopy.wait_send()
    xg1.wait_send()

    @pl.when(jnp.logical_not(selfcol))
    def _():
        xg0.wait_send()

    for i in range(NY):
        for q in range(2):
            cp_sib(q, i).wait_send()

    @pl.when(lax.rem(r, 2) == 0)
    def _():
        for i in range(NY):
            cp_plus(0, i, 0).wait_send()
            cp_plus(0, i, 1).wait_send()
            cp_minus(0, i, 0).wait_send()

    @pl.when(r == 0)
    def _():
        for i in range(NY):
            cp_minus(0, i, 1).wait_send()

    for s in range(4):
        for d in range(2):
            for i in range(CHUNKS):
                if s > 0 or i in firsts(d):
                    rs_copy(s, d, i).wait_send()
                if s < 3 or i in firsts(d):
                    ag_copy(s, d, i).wait_send()
    for k in range(NY):
        for q in range(2):
            sib_copy(q, seq[k], k).wait_send()

    @pl.when(lax.rem(r, 2) == 1)
    def _():
        for k in range(NY):
            z_copy(0, 0, k).wait_send()
            z_copy(0, 1, k).wait_send()
        z_cross(0, 0).wait_send()
        z_cross(0, 1).wait_send()

    @pl.when(lax.rem(r, 2) == 0)
    def _():
        for k in range(NY):
            z_copy(0, 2, k).wait_send()

    @pl.when(r == 2)
    def _():
        for k in range(NY):
            z_copy(0, 3, k).wait_send()

    @pl.when(r == 0)
    def _():
        z_cross(0, 2).wait_send()
        for k in range(1, NY):
            dt_copy(k).wait_send()

    @pl.when(jnp.logical_and(r == 0, xl != par))
    def _():
        dt_copy(0).wait_send()

    for i in range(CHUNKS):
        g_copy(i).wait_send()


def write_out(a_ref, b_ref, c_ref, ao_ref, bo_ref, co_ref, sem):
    copies = [
        pltpu.make_async_copy(src, dst, sem.at[i])
        for i, (src, dst) in enumerate(((c_ref, co_ref), (a_ref, ao_ref), (b_ref, bo_ref)))
    ]
    for copy in copies:
        copy.start()
    for copy in copies:
        copy.wait()


def body(tokens, codes, scales, d_hidden):
    t, dloc = tokens.shape
    _, wrows, group = codes.shape
    all2 = 2 * group
    codes_t = jnp.transpose(codes, (0, 2, 1))
    dh_t = jnp.transpose(d_hidden)
    dma = pltpu.SemaphoreType.DMA
    vm = pl.BlockSpec(memory_space=pltpu.VMEM)
    hid_t, dtok, grad_t = pl.pallas_call(
        kernel,
        out_shape=(
            jax.ShapeDtypeStruct((group, t), BF16),
            jax.ShapeDtypeStruct((t, dloc), BF16),
            jax.ShapeDtypeStruct((2, group, wrows), F32),
        ),
        in_specs=[pl.BlockSpec(memory_space=pltpu.HBM)] * 4,
        out_specs=(vm, vm, vm),
        scratch_shapes=[
            pltpu.VMEM((2, group, wrows), BF16),
            pltpu.VMEM(scales.shape, BF16),
            pltpu.VMEM((group, t), BF16),
            pltpu.SemaphoreType.DMA((4,)),
            pltpu.VMEM((t, dloc), BF16),
            pltpu.VMEM((4, NY, t, dloc), BF16),
            pltpu.VMEM((2, all2, wrows), BF16),
            pltpu.VMEM((2, wrows, all2), BF16),
            pltpu.VMEM((2, all2 // 2, t), BF16),
            pltpu.VMEM((2, 4, all2, t), BF16),
            pltpu.VMEM((2, all2, t), F32),
            pltpu.VMEM((all2, t), F32),
            pltpu.VMEM((NY, all2, t), BF16),
            pltpu.VMEM((2, all2, wrows), F32),
            pltpu.VMEM((4, NY, dloc, t), BF16),
            pltpu.VMEM((2, NY, dloc, t), BF16),
            pltpu.VMEM((4, NY, dloc, t), BF16),
            pltpu.VMEM((3, dloc, t), BF16),
            pltpu.VMEM((2, NY, dloc, t), BF16),
            pltpu.VMEM((2, dloc, t), BF16),
            pltpu.VMEM((all2, wrows), BF16),
            pltpu.VMEM((all2, wrows), BF16),
            dma(()),
            dma(()),
            dma(()),
            dma((2,)),
            dma((NY,)),
            dma((2, NY)),
            dma((NY,)),
            dma((2, NY)),
            dma((NY,)),
            dma((2, NY)),
            dma((2, NY)),
            dma((4, 2, CHUNKS)),
            dma((4, 2, CHUNKS)),
            dma((4, 2, CHUNKS)),
            dma((4, 2, CHUNKS)),
            dma((2, NY)),
            dma((2, NY)),
            dma((4, NY)),
            dma((4, NY)),
            dma((3,)),
            dma((3,)),
            dma((NY,)),
            dma((2,)),
            dma((CHUNKS,)),
            dma((CHUNKS,)),
        ],
        compiler_params=pltpu.CompilerParams(collective_id=0, has_side_effects=True, vmem_limit_bytes=24 * 1024 * 1024),
    )(*(pltpu.with_memory_space_constraint(a, pltpu.HBM) for a in (tokens, codes_t, scales, dh_t)))
    hid_t, dtok, grad_t = pl.pallas_call(
        write_out,
        out_shape=tuple(jax.ShapeDtypeStruct(a.shape, a.dtype) for a in (hid_t, dtok, grad_t)),
        in_specs=[vm] * 3,
        out_specs=(pl.BlockSpec(memory_space=pltpu.HBM),) * 3,
        scratch_shapes=[dma((3,))],
        compiler_params=pltpu.CompilerParams(vmem_limit_bytes=4 * 1024 * 1024),
    )(hid_t, dtok, grad_t)
    return (jnp.transpose(hid_t), dtok, jnp.transpose(grad_t, (0, 2, 1)))


def solution(mesh):
    return jax.shard_map(
        body,
        mesh=mesh,
        in_specs=(
            P("local", "node"),
            P(None, "local", "node"),
            P(None, "local", "node"),
            P("local", "node"),
        ),
        out_specs=(P("local", "node"), P("local", "node"), P(None, "local", "node")),
        check_vma=False,
    )
```

```python
import math

import jax
import jax.numpy as jnp
from jax import lax
from jax.experimental import pallas as pl
from jax.experimental.pallas import tpu as pltpu
from jax.sharding import PartitionSpec as P

MESH = pl.DeviceIdType.MESH
BLOCK = 128
NY = 8
NZ = 8
CHUNKS = 4
F32 = jnp.float32
BF16 = jnp.bfloat16


def dot_nn(a, b):
    return lax.dot_general(a, b, (((1,), (0,)), ((), ())), preferred_element_type=F32)


def dot_nt(a, b):
    return lax.dot_general(a, b, (((1,), (1,)), ((), ())), preferred_element_type=F32)


def kernel(
    tok_hbm,
    codes_hbm,
    scale_hbm,
    dh_hbm,
    hid_ref,
    dtok_ref,
    grad_ref,
    codes_ref,
    scale_ref,
    dh_ref,
    in_sem,
    xin,
    x,
    w,
    wt,
    rs0,
    rs,
    part,
    own,
    dg,
    acc,
    dp,
    sib,
    zin,
    zx,
    zsum,
    dtin,
    gsend,
    grecv,
    loc_sem,
    w_s,
    w_r,
    xg_s,
    xg_r,
    xp_s,
    xp_r,
    xm_s,
    xm_r,
    xs_s,
    xs_r,
    rs_s,
    rs_r,
    ag_s,
    ag_r,
    sb_s,
    sb_r,
    zo_s,
    zo_r,
    zx_s,
    zx_r,
    dt_s,
    dt_r,
    g_s,
    g_r,
):
    loads = [
        pltpu.make_async_copy(a, b, in_sem.at[i])
        for i, (a, b) in enumerate(
            ((tok_hbm, xin), (scale_hbm, scale_ref), (codes_hbm, codes_ref), (dh_hbm, dh_ref))
        )
    ]
    for load in loads:
        load.start()

    n = lax.axis_index("node")
    l = lax.axis_index("local")
    z = lax.div(n, 4)
    xl = lax.rem(lax.div(n, 2), 2)
    c = lax.rem(n, 2)
    h = lax.div(l, NY)
    y = lax.rem(l, NY)
    half = codes_ref.shape[1] // CHUNKS
    factor = 1.0 / math.sqrt(tok_hbm.shape[0] * 16)
    rows = 2 * half

    def dev(z_, xl_, c_, h_, y_):
        return (z_ * 4 + xl_ * 2 + c_, h_ * NY + y_)

    zu = lax.rem(z + 1, NZ)
    zd = lax.rem(z + NZ - 1, NZ)
    yu = lax.rem(y + 1, NY)
    yd = lax.rem(y + NY - 1, NY)
    zu2 = lax.rem(z + 2, NZ)
    zd2 = lax.rem(z + NZ - 2, NZ)
    up_z = dev(zu, xl, c, h, y)
    up_z2 = dev(zu2, xl, c, h, y)
    dn_z2 = dev(zd2, xl, c, h, y)
    dn_z = dev(zd, xl, c, h, y)
    up_y = dev(z, xl, c, h, yu)
    dn_y = dev(z, xl, c, h, yd)
    sibling = dev(z, xl, 1 - c, h, y)
    partner = dev(z, xl, c, 1 - h, y)
    other = 1 - c

    barrier = pltpu.get_barrier_semaphore()
    peers = [up_z, dn_z, up_z2, dn_z2, sibling, partner]
    cross = [dev(z_, xl, other, h, y) for z_ in (zd, zu, zd2, zu2)]
    peers += cross
    for dx in range(2):
        for dy in range(NY):
            if dx or dy:
                peers.append(dev(z, lax.rem(xl + dx, 2), c, h, lax.rem(y + dy, NY)))
    for peer in peers:
        pl.semaphore_signal(barrier, inc=1, device_id=peer, device_id_type=MESH)

    def remote(src, dst, ss, rr, to):
        return pltpu.make_async_remote_copy(
            src_ref=src, dst_ref=dst, send_sem=ss, recv_sem=rr, device_id=to, device_id_type=MESH
        )

    loads[0].wait()
    loads[3].wait()

    pl.semaphore_wait(barrier, len(peers))

    ystar = 2 * lax.rem(z, 4) + xl
    qsrc = lax.div(z, 4)
    myslot = x.at[2 * qsrc + c, y]
    own_col = dev(z, xl, c, h, ystar)
    oth_col = dev(z, 1 - xl, c, h, ystar)
    xg0 = remote(xin, myslot, xg_s.at[0], xg_r.at[y], own_col)
    xg1 = remote(xin, myslot, xg_s.at[1], xg_r.at[y], oth_col)
    xg1.start()
    selfcol = ystar == y

    @pl.when(selfcol)
    def _():
        pltpu.make_async_copy(xin, myslot, xg_r.at[y]).start()

    @pl.when(jnp.logical_not(selfcol))
    def _():
        xg0.start()

    loads[1].wait()
    loads[2].wait()
    pick = (
        lax.broadcasted_iota(jnp.int32, (2, 2 * BLOCK), 1) // BLOCK
        == lax.broadcasted_iota(jnp.int32, (2, 2 * BLOCK), 0)
    ).astype(BF16)
    for k in range(2):
        spread = lax.dot_general(
            scale_ref[k],
            pick,
            (((0,), (0,)), ((), ())),
            preferred_element_type=F32,
        )
        for i in range(CHUNKS):
            f = pl.ds(half * i, half)
            code = codes_ref[k, f, :].astype(F32)
            s = spread[half * i : half * (i + 1)]
            w[h, pl.ds(rows * i + half * k, half), :] = (code * s).astype(BF16)
    wcopy = remote(w.at[h], w.at[h], w_s, w_r, partner)
    wcopy.start()

    dz = lax.rem(z - lax.div(y, 2) + NZ, NZ)
    r = lax.rem(dz, 4)
    qo = lax.div(dz, 4)
    qp = lax.div(lax.rem(dz + 7, NZ), 4)
    qm = 1 - qp

    def block(d):
        return lax.rem(y + d + NY, NY)

    order = [block(d) for d in (4, 3, -3, 2, -2, 1, -1, 0)]

    def slot(q, tb):
        return x.at[2 * q + c, tb]

    def cp_plus(q, i, far):
        s = slot(q, order[i])
        return remote(s, s, xp_s.at[far, i], xp_r.at[i], up_z2 if far else up_z)

    def cp_minus(q, i, far):
        s = slot(q, order[i])
        return remote(s, s, xm_s.at[far, i], xm_r.at[i], dn_z2 if far else dn_z)

    def cp_sib(q, i):
        s = slot(q, order[i])
        return remote(s, s, xs_s.at[q, i], xs_r.at[q, i], sibling)

    def sib_wait(i):
        for q in range(2):
            s = x.at[2 * q + other, order[i]]
            remote(s, s, xs_s.at[q, i], xs_r.at[q, i], sibling).wait_recv()

    def spread_own(i):
        remote(xin, slot(qo, order[i]), xg_s.at[0], xg_r.at[order[i]], own_col).wait_recv()
        for far in (1, 0):
            cp_plus(qo, i, far).start()
            cp_minus(qo, i, far).start()
        cp_sib(qo, i).start()

    def take_plus(i):
        cp_plus(qp, i, 0).wait_recv()
        cp_sib(qp, i).start()

    def take_minus(i):
        cp_minus(qm, i, 0).wait_recv()
        cp_sib(qm, i).start()

    def relay(i):
        cp_plus(qp, i, 0).wait_recv()
        cp_plus(qp, i, 1).start()
        cp_plus(qp, i, 0).start()
        cp_sib(qp, i).start()
        cp_minus(qm, i, 0).wait_recv()
        cp_minus(qm, i, 0).start()
        cp_sib(qm, i).start()

    stages = ((0,), (1, 2), (3, 4), (5, 6, 7))
    early = ((0, 1, 2), (3, 4), (5, 6), (7,))
    ahead = ((0, 1, 2), (3,), (), ())

    def tokens_stage(t):
        @pl.when(r == 0)
        def _():
            if t == 0:
                for i in range(NY):
                    spread_own(i)
            for i in stages[t]:
                take_plus(i)

        @pl.when(r == 1)
        def _():
            for i in early[t]:
                take_plus(i)
            for i in stages[t]:
                take_minus(i)

        @pl.when(r == 2)
        def _():
            for i in ahead[t]:
                relay(i)

        @pl.when(r == 3)
        def _():
            for i in early[t]:
                take_minus(i)
            for i in stages[t]:
                take_plus(i)

        for i in stages[t]:
            sib_wait(i)

    tokens_stage(0)
    remote(w.at[1 - h], w.at[1 - h], w_s, w_r, partner).wait_recv()

    def xq(q, tb):
        return jnp.concatenate([x[2 * q, tb], x[2 * q + 1, tb]], axis=1)

    def partial(tb, lo, hi):
        a = slice(lo * rows, hi * rows)
        return dot_nt(w[0, a, :], xq(0, tb)) + dot_nt(w[1, a, :], xq(1, tb))

    def ch(i):
        return pl.ds(rows * i, rows)

    nbr = (up_y, dn_y)
    hc = CHUNKS // 2

    def rs_copy(s, d, i):
        src = rs0.at[d, ch(i - hc * d)] if s == 0 else rs.at[d, s - 1, ch(i)]
        return remote(src, rs.at[d, s, ch(i)], rs_s.at[s, d, i], rs_r.at[s, d, i], nbr[d])

    def firsts(d):
        return range(hc) if d == 0 else range(hc, CHUNKS)

    for d in range(2):
        rs0[d] = partial(block(4), d * hc, (d + 1) * hc).astype(BF16)
        for i in firsts(d):
            rs_copy(0, d, i).start()
    for s in range(1, 4):
        tokens_stage(s)
        for d in range(2):
            part[d] = partial(block(4 - s if d == 0 else s - 4), 0, CHUNKS)
            if s == 1:
                for i in firsts(1 - d):
                    rs[d, 0, ch(i)] = part[d, ch(i)].astype(BF16)
                    rs_copy(1, d, i).start()
        for i in range(CHUNKS):
            for d in range(2):
                if s == 1:
                    if i not in firsts(d):
                        continue
                rs_copy(s - 1, d, i).wait_recv()
                rs[d, s - 1, ch(i)] = (rs[d, s - 1, ch(i)].astype(F32) + part[d, ch(i)]).astype(BF16)
                rs_copy(s, d, i).start()
            nxt = {(1, 0): 4, (1, 2): 5, (2, 0): 6, (2, 2): 7}.get((s, i))
            if nxt is not None:

                @pl.when(r == 2)
                def _():
                    relay(nxt)

    own[...] = partial(y, 0, CHUNKS)

    def ag_copy(s, d, i):
        b = lax.rem(y + (NY - s if d == 0 else s), NY)
        sl = dg.at[b, ch(i)]
        return remote(sl, sl, ag_s.at[s, d, i], ag_r.at[s, d, i], nbr[d])

    def ag_wait(s, d, i):
        b = lax.rem(y + (NY - 1 - s if d == 0 else s + 1), NY)
        sl = dg.at[b, ch(i)]
        remote(sl, sl, ag_s.at[s, d, i], ag_r.at[s, d, i], nbr[d]).wait_recv()

    for i in range(CHUNKS):
        for d in range(2):
            rs_copy(3, d, i).wait_recv()
        tot = own[ch(i)] + rs[0, 3, ch(i)].astype(F32) + rs[1, 3, ch(i)].astype(F32)
        gate, up = tot[:half], tot[half:]
        f = pl.ds(half * i, half)
        sg = jax.nn.sigmoid(gate)
        act = gate * sg
        hid_ref[f, :] = (act * up).astype(BF16)
        gin = dh_ref[f, :].astype(F32)
        dgate = (gin * up * sg * (1.0 + gate * (1.0 - sg))).astype(BF16)
        dup = (gin * act).astype(BF16)
        dg[y, pl.ds(rows * i, half), :] = dgate
        dg[y, pl.ds(rows * i + half, half), :] = dup
        for d in range(2):
            ag_copy(0, d, i).start()

    for q in range(2):
        wt[q] = jnp.transpose(w[q])

    def grads_of(blocks, first):
        a = jnp.concatenate([dg[b] for b in blocks], axis=1) if len(blocks) > 1 else dg[blocks[0]]
        for j in range(4):
            xs = [x[j, b] for b in blocks]
            bb = jnp.concatenate(xs, axis=0) if len(blocks) > 1 else xs[0]
            v = dot_nn(a, bb)
            col = slice(128 * (j % 2), 128 * (j % 2) + 128)
            if first:
                acc[j // 2, :, col] = v
            else:
                acc[j // 2, :, col] = acc[j // 2, :, col] + v

    def sib_copy(q, b, k):
        return remote(
            dp.at[2 * q + other, b], sib.at[q, k], sb_s.at[q, k], sb_r.at[q, k], sibling
        )

    def inputs_of(b, k):
        for q in range(2):
            v = dot_nn(wt[q], dg[b]).astype(BF16)
            dp[2 * q, b] = v[:128]
            dp[2 * q + 1, b] = v[128:]
        if k == 7:
            last_leaves()
        for q in range(2):
            sib_copy(q, b, k).start()

    seq = [block(d) for d in (0, -1, 1, -2, 2, -3, 3, 4)]
    groups = ((0,), (1, 2), (3, 4), (5, 6), (7,))
    par = lax.rem(y, 2)

    z_to = (dn_z, up_z, dn_z2, up_z2)

    def z_copy(q, w_, k):
        return remote(zsum.at[q, k], zin.at[w_, k], zo_s.at[w_, k], zo_r.at[w_, k], z_to[w_])

    def z_add(q, ways, k, crossed=()):
        v = zsum[q, k].astype(F32)
        for w_ in ways:
            z_copy(q, w_, k).wait_recv()
            v = v + zin[w_, k].astype(F32)
        for w_ in crossed if k == 7 else ():
            z_cross(q, w_).wait_recv()
            v = v + zx[w_].astype(F32)
        zsum[q, k] = v.astype(BF16)

    def dt_copy(k):
        return remote(
            zsum.at[qo, k], dtin.at[xl], dt_s.at[k], dt_r.at[xl], dev(z, par, c, h, seq[k])
        )

    def z_direct(q, w_):
        return remote(
            dp.at[2 * q + c, seq[7]], zin.at[w_, 7], zo_s.at[w_, 7], zo_r.at[w_, 7], z_to[w_]
        )

    def z_cross(q, w_):
        return remote(
            dp.at[2 * q + other, seq[7]], zx.at[w_], zx_s.at[w_], zx_r.at[w_], cross[w_]
        )

    def last_leaves():
        @pl.when(lax.rem(r, 2) == 1)
        def _():
            for q, w_ in ((qp, 0), (qm, 1)):
                z_direct(q, w_).start()
                z_cross(q, w_).start()

        @pl.when(r == 0)
        def _():
            z_direct(qp, 2).start()
            z_cross(qp, 2).start()

    def cores(g):
        for k in groups[g]:
            for q in range(2):
                sib_copy(q, seq[k], k).wait_recv()
                v = dp[2 * q + c, seq[k]].astype(F32) + sib[q, k].astype(F32)
                zsum[q, k] = v.astype(BF16)

            if k == 7:
                continue

            @pl.when(lax.rem(r, 2) == 1)
            def _():
                z_copy(qp, 0, k).start()
                z_copy(qm, 1, k).start()

            @pl.when(r == 0)
            def _():
                z_copy(qp, 2, k).start()

    def middle(g):
        @pl.when(r == 2)
        def _():
            for k in groups[g]:
                z_add(qp, (0, 2), k, (0, 2))
                z_copy(qp, 2, k).start()
                z_add(qm, (1,), k, (1,))
                z_copy(qm, 3, k).start()

    def collect(g):
        @pl.when(r == 0)
        def _():
            for k in groups[g]:
                z_add(qo, (0, 1, 2, 3), k, (0, 1))
                if k > 0:
                    dt_copy(k).start()
                else:

                    @pl.when(xl == par)
                    def _():
                        pltpu.make_async_copy(zsum.at[qo, 0], dtin.at[xl], dt_r.at[xl]).start()

                    @pl.when(xl != par)
                    def _():
                        dt_copy(0).start()

    inputs_of(seq[0], 0)
    grads_of([seq[0]], True)
    def g_copy(i):
        return remote(gsend.at[ch(i)], grecv.at[ch(i)], g_s.at[i], g_r.at[i], partner)

    for s in range(1, 4):
        for i in range(CHUNKS):
            for d in range(2):
                ag_wait(s - 1, d, i)
                if s < 3 or i in firsts(d):
                    ag_copy(s, d, i).start()
            if i == 1:
                cores(s - 1)
        for k in groups[s]:
            inputs_of(seq[k], k)
        grads_of([seq[k] for k in groups[s]], False)
        middle(s - 1)
        if s > 1:
            collect(s - 2)

    def send_grads(i):
        pair = jnp.concatenate([x[2 * (1 - h) + j, seq[7]] for j in range(2)], axis=1)
        v = dot_nn(dg[seq[7], ch(i)], pair)
        gsend[ch(i)] = (acc[1 - h, ch(i)] + v).astype(BF16)
        g_copy(i).start()

    for i in range(hc):
        ag_wait(3, 0, i)
        ag_wait(3, 1, i + hc)
        if i == hc - 1:
            inputs_of(seq[7], 7)
        send_grads(i)
        send_grads(i + hc)
        if i == 0:
            cores(3)
    collect(2)
    cores(4)
    middle(3)
    middle(4)
    collect(3)
    collect(4)
    for j in range(2):
        col = slice(128 * j, 128 * j + 128)
        acc[h, :, col] = acc[h, :, col] + dot_nn(dg[seq[7]], x[2 * h + j, seq[7]])

    for i in range(CHUNKS):
        g_copy(i).wait_recv()
        for k in range(2):
            a = pl.ds(rows * i + half * k, half)
            grad_ref[k, pl.ds(half * i, half), :] = (
                acc[h, a, :] + grecv[a, :].astype(F32)
            ) * factor

    for s in range(2):
        remote(zsum.at[0, 0], dtin.at[s], dt_s.at[0], dt_r.at[s], sibling).wait_recv()
    tot = dtin[0].astype(F32) + dtin[1].astype(F32)
    dtok_ref[...] = jnp.transpose(tot).astype(BF16)

    wcopy.wait_send()
    xg1.wait_send()

    @pl.when(jnp.logical_not(selfcol))
    def _():
        xg0.wait_send()

    for i in range(NY):
        for q in range(2):
            cp_sib(q, i).wait_send()

    @pl.when(lax.rem(r, 2) == 0)
    def _():
        for i in range(NY):
            cp_plus(0, i, 0).wait_send()
            cp_plus(0, i, 1).wait_send()
            cp_minus(0, i, 0).wait_send()

    @pl.when(r == 0)
    def _():
        for i in range(NY):
            cp_minus(0, i, 1).wait_send()

    for s in range(4):
        for d in range(2):
            for i in range(CHUNKS):
                if s > 0 or i in firsts(d):
                    rs_copy(s, d, i).wait_send()
                if s < 3 or i in firsts(d):
                    ag_copy(s, d, i).wait_send()
    for k in range(NY):
        for q in range(2):
            sib_copy(q, seq[k], k).wait_send()

    @pl.when(lax.rem(r, 2) == 1)
    def _():
        for k in range(NY):
            z_copy(0, 0, k).wait_send()
            z_copy(0, 1, k).wait_send()
        z_cross(0, 0).wait_send()
        z_cross(0, 1).wait_send()

    @pl.when(lax.rem(r, 2) == 0)
    def _():
        for k in range(NY):
            z_copy(0, 2, k).wait_send()

    @pl.when(r == 2)
    def _():
        for k in range(NY):
            z_copy(0, 3, k).wait_send()

    @pl.when(r == 0)
    def _():
        z_cross(0, 2).wait_send()
        for k in range(1, NY):
            dt_copy(k).wait_send()

    @pl.when(jnp.logical_and(r == 0, xl != par))
    def _():
        dt_copy(0).wait_send()

    for i in range(CHUNKS):
        g_copy(i).wait_send()


def write_out(a_ref, b_ref, c_ref, ao_ref, bo_ref, co_ref, sem):
    copies = [
        pltpu.make_async_copy(src, dst, sem.at[i])
        for i, (src, dst) in enumerate(((c_ref, co_ref), (a_ref, ao_ref), (b_ref, bo_ref)))
    ]
    for copy in copies:
        copy.start()
    for copy in copies:
        copy.wait()


def body(tokens, codes, scales, d_hidden):
    t, dloc = tokens.shape
    _, wrows, group = codes.shape
    all2 = 2 * group
    codes_t = jnp.transpose(codes, (0, 2, 1))
    dh_t = jnp.transpose(d_hidden)
    dma = pltpu.SemaphoreType.DMA
    vm = pl.BlockSpec(memory_space=pltpu.VMEM)
    hid_t, dtok, grad_t = pl.pallas_call(
        kernel,
        out_shape=(
            jax.ShapeDtypeStruct((group, t), BF16),
            jax.ShapeDtypeStruct((t, dloc), BF16),
            jax.ShapeDtypeStruct((2, group, wrows), F32),
        ),
        in_specs=[pl.BlockSpec(memory_space=pltpu.HBM)] * 4,
        out_specs=(vm, vm, vm),
        scratch_shapes=[
            pltpu.VMEM((2, group, wrows), BF16),
            pltpu.VMEM(scales.shape, BF16),
            pltpu.VMEM((group, t), BF16),
            pltpu.SemaphoreType.DMA((4,)),
            pltpu.VMEM((t, dloc), BF16),
            pltpu.VMEM((4, NY, t, dloc), BF16),
            pltpu.VMEM((2, all2, wrows), BF16),
            pltpu.VMEM((2, wrows, all2), BF16),
            pltpu.VMEM((2, all2 // 2, t), BF16),
            pltpu.VMEM((2, 4, all2, t), BF16),
            pltpu.VMEM((2, all2, t), F32),
            pltpu.VMEM((all2, t), F32),
            pltpu.VMEM((NY, all2, t), BF16),
            pltpu.VMEM((2, all2, wrows), F32),
            pltpu.VMEM((4, NY, dloc, t), BF16),
            pltpu.VMEM((2, NY, dloc, t), BF16),
            pltpu.VMEM((4, NY, dloc, t), BF16),
            pltpu.VMEM((3, dloc, t), BF16),
            pltpu.VMEM((2, NY, dloc, t), BF16),
            pltpu.VMEM((2, dloc, t), BF16),
            pltpu.VMEM((all2, wrows), BF16),
            pltpu.VMEM((all2, wrows), BF16),
            dma(()),
            dma(()),
            dma(()),
            dma((2,)),
            dma((NY,)),
            dma((2, NY)),
            dma((NY,)),
            dma((2, NY)),
            dma((NY,)),
            dma((2, NY)),
            dma((2, NY)),
            dma((4, 2, CHUNKS)),
            dma((4, 2, CHUNKS)),
            dma((4, 2, CHUNKS)),
            dma((4, 2, CHUNKS)),
            dma((2, NY)),
            dma((2, NY)),
            dma((4, NY)),
            dma((4, NY)),
            dma((3,)),
            dma((3,)),
            dma((NY,)),
            dma((2,)),
            dma((CHUNKS,)),
            dma((CHUNKS,)),
        ],
        compiler_params=pltpu.CompilerParams(collective_id=0, has_side_effects=True, vmem_limit_bytes=24 * 1024 * 1024),
    )(*(pltpu.with_memory_space_constraint(a, pltpu.HBM) for a in (tokens, codes_t, scales, dh_t)))
    hid_t, dtok, grad_t = pl.pallas_call(
        write_out,
        out_shape=tuple(jax.ShapeDtypeStruct(a.shape, a.dtype) for a in (hid_t, dtok, grad_t)),
        in_specs=[vm] * 3,
        out_specs=(pl.BlockSpec(memory_space=pltpu.HBM),) * 3,
        scratch_shapes=[dma((3,))],
        compiler_params=pltpu.CompilerParams(vmem_limit_bytes=4 * 1024 * 1024),
    )(hid_t, dtok, grad_t)
    return (jnp.transpose(hid_t), dtok, jnp.transpose(grad_t, (0, 2, 1)))


def solution(mesh):
    return jax.shard_map(
        body,
        mesh=mesh,
        in_specs=(
            P("local", "node"),
            P(None, "local", "node"),
            P(None, "local", "node"),
            P("local", "node"),
        ),
        out_specs=(P("local", "node"), P("local", "node"), P(None, "local", "node")),
        check_vma=False,
    )
```
